512 devices in a mesh: chan: 16 (over x, y_hi, core), tm: 32 (over z, y_lo).
Axes of the slice: x: 4, y: 8 (y_hi: 2, y_lo: 4; y = y_hi * 4 + y_lo), z: 8, core: 2. Of those that a mesh axis runs over, the one named last changes fastest.
Arguments:
- records: bfloat16 [2048, 491520], P('chan', 'tm'), may hold values from -6 to 6
- fir_taps: bfloat16 [257], replicated, may hold values from -0.375 to 0.375
- partners: int32 [1, 16], replicated, may hold values from 0 to 15, as said below
Outputs:
- cross: float32 [1, 2048, 6144], P(None, 'chan', 'tm')
The draws below stay inside these ranges and needn't reach their ends.
Inputs may be any that keep to these rules, and one draw needn't show every extreme that they name: `partners`: each row is a permutation of the 16 blocks.
All inputs are finite; a program needn't handle non-finite values.
Results may differ from the reference program's by a relative error of at most 0.0003.
Values may be sent and summed in bfloat16 or wider, within the bound.
A program may use at most 64 MiB of HBM per device.

```python
import math
import jax
import jax.numpy as jnp
from jax import lax

CHD = 128
WIN = 2560
TAPS = 257
NBIN = 24
ROUNDS = 1
HOP = 1280
HALF = 128
NBLK = 16
CHANNELS = 2048
SAMPLES = 491520
WINDOWS = 384


def draw_partners(key, part):
    rows = []
    for round_index in range(ROUNDS):
        round_key = jax.random.fold_in(key, 7919 + round_index)
        perm_key, pick_key = jax.random.split(round_key)
        order = jax.random.permutation(perm_key, NBLK).astype(jnp.int32)
        picked = jax.random.randint(pick_key, (), 0, NBLK, dtype=jnp.int32)
        target = (picked + NBLK // 2) % NBLK
        places = jnp.arange(NBLK, dtype=jnp.int32)
        where_target = jnp.sum(jnp.where(order == target, places, 0)).astype(jnp.int32)
        moved = order[picked]
        order = order.at[where_target].set(moved)
        order = order.at[picked].set(target)
        rows.append(order)
    return jnp.stack(rows).astype(jnp.int32)


def steps_of(own_key, shape, cuts, smallest, high):
    factor_of = 1.0
    for axis_at, shards_of in cuts:
        heights = jax.random.uniform(jax.random.fold_in(jax.random.fold_in(own_key, 6), axis_at), (shards_of,), jnp.float32, smallest / len(cuts), high / len(cuts))
        factor_of = factor_of * jnp.repeat(jnp.exp(heights), shape[axis_at] // shards_of).reshape((-1,) + (1,) * (len(shape) - 1 - axis_at))
    return factor_of


def scatter_about(stream_key, extent, deviation, most, cuts=(), kind=jnp.bfloat16):
    gain = steps_of(stream_key, extent, cuts, -0.22, 0.18) if cuts else 1.0
    array = jax.random.normal(stream_key, extent, jnp.float32) * deviation * gain
    return jnp.minimum(jnp.maximum(array, -most), most).astype(kind)


def setup_inputs(seed: int = 0) -> dict:
    keys = jax.random.split(jax.random.key(seed), 4)
    records = scatter_about(keys[0], (CHANNELS, SAMPLES), 1.0, 6.0, ((0, 16), (1, 32)))
    fir_taps = scatter_about(keys[1], (TAPS,), TAPS ** -0.5, 0.375)
    partners = draw_partners(jax.random.fold_in(keys[3], 71), 0)
    return {"records": records, "fir_taps": fir_taps, "partners": partners}


first_bin = 4

def toeplitz(fir_taps):
    width = fir_taps.shape[0] - 1
    padded = jnp.concatenate([jnp.zeros((width,), fir_taps.dtype), fir_taps, jnp.zeros((width - 1,), fir_taps.dtype)])
    rolled = jnp.concatenate([padded[width:], padded[:width]])
    flat = jnp.tile(rolled, width)[:width * (3 * width - 1)]
    skewed = flat.reshape(width, 3 * width - 1)[:, :2 * width]
    return skewed.T

def fourier_basis(win_len, tap_half, bins):
    times = jnp.arange(win_len, dtype=jnp.int32)
    freqs = jnp.arange(bins, dtype=jnp.int32) + first_bin
    phase_int = freqs[None, :] * times[:, None] % win_len
    angle = 2.0 * math.pi / win_len * phase_int.astype(jnp.float32)
    edge = jnp.minimum(times, win_len - 1 - times)
    ramp = jnp.sin(math.pi * (edge.astype(jnp.float32) + 0.5) / (2.0 * tap_half))
    taper = jnp.where(edge < tap_half, ramp * ramp, jnp.float32(1.0))
    scale = taper[:, None] / math.sqrt(win_len)
    return jnp.concatenate([scale * jnp.cos(angle), -scale * jnp.sin(angle)], axis=1)

def whiten(spectra, bins):
    real_part = spectra[..., :bins]
    imag_part = spectra[..., bins:]
    amplitude = jnp.sqrt(real_part * real_part + imag_part * imag_part + 1.0)
    return spectra / jnp.concatenate([amplitude, amplitude], axis=-1)

def cross_terms(left_spec, right_spec, bins):
    hi = lax.Precision.HIGHEST
    left_real, left_imag = (left_spec[..., :bins], left_spec[..., bins:])
    right_real, right_imag = (right_spec[..., :bins], right_spec[..., bins:])
    real_real = jnp.einsum('iwf,jwf->ijf', left_real, right_real, precision=hi)
    imag_imag = jnp.einsum('iwf,jwf->ijf', left_imag, right_imag, precision=hi)
    imag_real = jnp.einsum('iwf,jwf->ijf', left_imag, right_real, precision=hi)
    real_imag = jnp.einsum('iwf,jwf->ijf', left_real, right_imag, precision=hi)
    joined = jnp.stack([real_real + imag_imag, imag_real - real_imag], axis=2)
    return joined.reshape(left_spec.shape[0], right_spec.shape[0] * 2 * bins)

def reference(records, fir_taps, partners):
    hi = lax.Precision.HIGHEST
    toeplitz_mat = toeplitz(fir_taps).astype(jnp.float32)
    basis = fourier_basis(WIN, HALF, NBIN)
    block_len = 2 * HALF
    block_count = (SAMPLES + HOP) // block_len

    def block_spectra(block_rows):
        extended = jnp.pad(block_rows.astype(jnp.float32), ((0, 0), (HALF, HALF + HOP)))
        pieces = extended.reshape(CHD, block_count + 1, block_len)
        stacked_in = jnp.concatenate([pieces[:, :-1], pieces[:, 1:]], axis=2)
        filtered = jnp.einsum('cnu,uv->cnv', stacked_in, toeplitz_mat, precision=hi)
        by_hop = filtered.reshape(CHD, WINDOWS + 1, HOP)
        spectra = jnp.einsum('cwt,tq->cwq', by_hop[:, :-1], basis[:HOP], precision=hi)
        spectra = spectra + jnp.einsum('cwt,tq->cwq', by_hop[:, 1:], basis[HOP:], precision=hi)
        return whiten(spectra, NBIN)
    all_spec = lax.map(block_spectra, records.reshape(NBLK, CHD, SAMPLES))
    scale = 1.0 / math.sqrt(WINDOWS)

    def one_round(partner_row):

        def one_block(block_id):
            partner_id = partner_row[block_id]
            return cross_terms(all_spec[block_id], all_spec[partner_id], NBIN) * scale
        return lax.map(one_block, jnp.arange(NBLK, dtype=jnp.int32))
    result = lax.map(one_round, partners)
    return result.reshape(ROUNDS, CHANNELS, CHD * 2 * NBIN)
```

```python
import functools
import math

import jax
import jax.numpy as jnp
import ml_dtypes
import numpy as np
from jax import lax
from jax.experimental import pallas as pl
from jax.experimental.pallas import tpu as pltpu
from jax.sharding import PartitionSpec as P

WIN = 2560
HOP = WIN // 2
NBIN = 24
HALF = 128
FIRST_BIN = 4
NQ = 2 * NBIN
CH = 128
LWIN = 12
ROWS = NBIN * 2 * LWIN
SPEC = 608
NX, NYH, NC = 4, 2, 2
NZ, NYL = 8, 4
NTM = NZ * NYL
JS = CH // NZ
GROUP = 3 * 2 * LWIN
PIECE = GROUP + 2 * LWIN
KDIM = NZ * 2 * LWIN
MESH = pl.DeviceIdType.MESH
NT = (((1,), (1,)), ((), ()))


def basis_table():
    t = np.arange(WIN)
    edge = np.minimum(t, WIN - 1 - t)
    ramp = np.sin(math.pi * (edge + 0.5) / (2.0 * HALF))
    taper = np.where(edge < HALF, ramp * ramp, 1.0) / math.sqrt(WIN)
    phase = (np.arange(NBIN)[:, None] + FIRST_BIN) * t[None, :] % WIN
    angle = 2.0 * math.pi / WIN * phase
    table = np.concatenate([np.cos(angle), -np.sin(angle)], axis=0) * taper
    table = np.pad(table, ((0, 0), (2 * HALF, 2 * HALF))).astype(np.float32)
    high = table.astype(ml_dtypes.bfloat16)
    low = (table - high.astype(np.float32)).astype(ml_dtypes.bfloat16)
    return np.concatenate([high, low], axis=0)


def split(value):
    high = value.astype(jnp.bfloat16)
    return high, (value - high.astype(jnp.float32)).astype(jnp.bfloat16)


def to_f32(codes):
    return codes.astype(jnp.int32).astype(jnp.float32)


def to_i16(value):
    return value.astype(jnp.int32).astype(jnp.int16)


def kernel(
    partners, taps, basis_hbm, x_hbm, out_ref,
    xs, basis, d_op, e_first, e_last, acc, up_send, low_send, up_recv, low_recv,
    coded, chan_got, z_got, a_val, sis_send, sis_recv, piece_send, piece_got,
    e_op, part_sum, part_got, flat, turned,
    x_sem, basis_sem, send_sem, recv_sem,
):
    ci, ti = lax.axis_index("chan"), lax.axis_index("tm")
    x, yh, core = ci // 4, (ci // 2) % 2, ci % 2
    z, yl = ti // NYL, ti % NYL

    def chan_id(xx, yy, cc):
        return (xx * 2 + yy) * 2 + cc

    def at_x(step):
        return (chan_id((x + step + NX) % NX, yh, core), ti)

    def at_z(step):
        return (ci, ((z + step + NZ) % NZ) * NYL + yl)

    def at_yl(step):
        return (ci, z * NYL + (yl + step) % NYL)

    def at_tm(step):
        return (ci, (ti + step + NTM) % NTM)

    across = (chan_id(x, 1 - yh, core), ti)
    sister = (chan_id(x, yh, 1 - core), ti)

    fetch_basis = pltpu.make_async_copy(basis_hbm, basis, basis_sem)
    fetch_basis.start()
    pair_order = [0, 5, 1, 2, 3, 4]

    def fetch(p):
        cols = pl.ds(2 * HOP * p, 2 * HOP)
        return pltpu.make_async_copy(x_hbm.at[:, cols], xs.at[:, cols], x_sem.at[p])

    for p in pair_order:
        fetch(p).start()

    barrier = pltpu.get_barrier_semaphore()
    peers = [at_tm(1), at_tm(-1), across, sister, at_x(1), at_x(-1)]
    peers += [at_z(d) for d in range(1, NZ)] + [at_yl(e) for e in range(1, NYL)]
    for peer in peers:
        pl.semaphore_signal(barrier, inc=1, device_id=peer, device_id_type=MESH)

    counter = [0]

    def send(src, dst, device):
        slot = counter[0]
        counter[0] += 1
        copy = pltpu.make_async_remote_copy(
            src_ref=src, dst_ref=dst, send_sem=send_sem.at[slot], recv_sem=recv_sem.at[slot],
            device_id=device, device_id_type=MESH,
        )
        copy.start()
        return copy

    sent = []

    acc[...] = jnp.zeros_like(acc)
    toep = pltpu.roll(jnp.broadcast_to(taps[...], (512, 512)), 0, 1, stride=1, stride_axis=0)
    toep = toep[:, :256].astype(jnp.bfloat16)
    fetch_basis.wait()
    for i in range(11):
        both = jnp.dot(
            basis[:, 256 * i : 256 * i + 512], toep, preferred_element_type=jnp.float32
        )
        high, low = split(both[:NQ] + both[NQ:])
        for half in range(2):
            j = 2 * i + half
            h_part = high[:, 128 * half : 128 * half + 128]
            l_part = low[:, 128 * half : 128 * half + 128]
            if j == 0:
                e_last[:NQ, :] = h_part
                e_last[NQ:, :] = l_part
            elif j == 21:
                e_first[:NQ, :] = h_part
                e_first[NQ:, :] = l_part
            else:
                row = 0 if j <= 10 else 2 * NQ
                col = 128 * ((j - 1) % 10)
                d_op[row : row + NQ, col : col + 128] = h_part
                d_op[row + NQ : row + 2 * NQ, col : col + 128] = l_part

    def hop_pair(p):
        fetch(p).wait()
        base = pl.multiple_of(2 * HOP * p, 128)
        second = pl.multiple_of(2 * HOP * p + HOP, 128)
        tail_a = pl.multiple_of(2 * HOP * p + HOP - 128, 128)
        tail_b = pl.multiple_of(2 * HOP * p + 2 * HOP - 128, 128)

        def both_hops(first, other, width):
            return jnp.concatenate([xs[:, pl.ds(first, width)], xs[:, pl.ds(other, width)]], axis=0)

        def product(left, right):
            return lax.dot_general(left, right, NT, preferred_element_type=jnp.float32)

        main = product(d_op[...], both_hops(base, second, HOP))
        first = product(e_first[...], both_hops(base, second, 128))
        last = product(e_last[...], both_hops(tail_a, tail_b, 128))
        p0 = main[:NQ] + main[NQ : 2 * NQ]
        p1 = main[2 * NQ : 3 * NQ] + main[3 * NQ :]
        p2 = first[:NQ] + first[NQ:]
        p3 = last[:NQ] + last[NQ:]
        for hop in range(2):
            lanes = slice(128 * hop, 128 * hop + 128)
            at = 2 * p + hop
            acc[at] += p2[:, lanes]
            acc[at + 1] += p1[:, lanes]
            acc[at + 2] += p0[:, lanes]
            acc[at + 3] += p3[:, lanes]

    hop_pair(0)
    hop_pair(5)
    up_send[...] = acc[0:2]
    low_send[...] = acc[14]
    pl.semaphore_wait(barrier, len(peers))
    up = send(up_send, up_recv, at_tm(-1))
    low = send(low_send, low_recv, at_tm(1))
    sent += [up, low]
    pl.loop(1, 5)(hop_pair)

    limit = jnp.float32(32767.0)

    def whiten(w):
        spec = acc[w + 2]
        real, imag = spec[:NBIN], spec[NBIN:]
        amp = jnp.sqrt(real * real + imag * imag + 1.0)
        real, imag = real / amp, imag / amp
        top = jnp.max(jnp.maximum(jnp.abs(real), jnp.abs(imag)), axis=0, keepdims=True)
        power = jnp.ceil(jnp.log2(jnp.maximum(top, 1e-30)))
        gain = limit / jnp.exp2(power)
        for part, value in enumerate((real, imag)):
            code = jnp.clip(jnp.floor(value * gain + 0.5), -limit, limit)
            coded[pl.ds(part * LWIN + w, NBIN, stride=2 * LWIN), :] = code
        coded[ROWS + w : ROWS + w + 1, :] = power
        coded[ROWS + LWIN + w : ROWS + LWIN + w + 1, :] = power

    for w in range(1, 10):
        whiten(w)
    coded[ROWS + 2 * LWIN :, :] = jnp.zeros((SPEC - ROWS - 2 * LWIN, CH), jnp.float32)
    up.wait_recv()
    low.wait_recv()
    acc[2] += jnp.where(ti > 0, 1.0, 0.0) * low_recv[...]
    acc[12:14] += jnp.where(ti < NTM - 1, 1.0, 0.0) * up_recv[...]
    for w in (0, 10, 11):
        whiten(w)
    own = chan_got.at[0]
    for r in range(0, SPEC, 32):
        chan_got[0, r : r + 32] = to_i16(coded[r : r + 32])

    def unpack_a(d, source, index):
        scale = jnp.exp2(to_f32(source[index, ROWS : ROWS + 32])[: 2 * LWIN]) * (1.0 / 32767.0)
        for i in range(NBIN // 2):
            block = to_f32(source[index, 48 * i : 48 * i + 48])
            a_val[2 * i, 24 * d : 24 * d + 24] = block[:24] * scale
            a_val[2 * i + 1, 24 * d : 24 * d + 24] = block[24:] * scale

    cut = SPEC // 2
    top, bottom = pl.ds(0, cut), pl.ds(cut, cut)

    def chan_slot(dx, dy):
        return chan_got.at[2 * dx + dy]

    y_top = send(own.at[top], chan_slot(0, 1).at[top], across)
    y_bottom = send(own.at[bottom], chan_slot(0, 1).at[bottom], across)
    x_right = send(own, chan_slot(1, 0), at_x(1))
    x_left = send(own, chan_slot(3, 0), at_x(-1))
    right = send(own, z_got.at[1], at_z(1))
    left = send(own, z_got.at[7], at_z(-1))
    sent += [y_top, y_bottom, x_right, x_left, right, left]
    unpack_a(0, chan_got, 0)

    def ring_step(step, right, left):
        right.wait_recv()
        left.wait_recv()
        if step < 3:
            right = send(z_got.at[step], z_got.at[step + 1], at_z(1))
            left = send(z_got.at[8 - step], z_got.at[7 - step], at_z(-1))
        else:
            right = send(z_got.at[3, top], z_got.at[4, top], at_z(1))
            left = send(z_got.at[5, bottom], z_got.at[4, bottom], at_z(-1))
        sent.extend([right, left])
        unpack_a(step, z_got, step)
        unpack_a(8 - step, z_got, 8 - step)
        return right, left

    x_right.wait_recv()
    x_left.wait_recv()
    far_top = send(chan_slot(1, 0).at[top], chan_slot(2, 0).at[top], at_x(1))
    far_bottom = send(chan_slot(3, 0).at[bottom], chan_slot(2, 0).at[bottom], at_x(-1))
    sent += [far_top, far_bottom]
    right, left = ring_step(1, right, left)
    right, left = ring_step(2, right, left)

    y_top.wait_recv()
    right_top = send(chan_slot(0, 1).at[top], chan_slot(1, 1).at[top], at_x(1))
    left_top = send(chan_slot(0, 1).at[top], chan_slot(3, 1).at[top], at_x(-1))
    y_bottom.wait_recv()
    right_bottom = send(chan_slot(0, 1).at[bottom], chan_slot(1, 1).at[bottom], at_x(1))
    left_bottom = send(chan_slot(0, 1).at[bottom], chan_slot(3, 1).at[bottom], at_x(-1))
    sent += [right_top, left_top, right_bottom, left_bottom]
    right, left = ring_step(3, right, left)
    right_top.wait_recv()
    across_top = send(chan_slot(1, 1).at[top], chan_slot(2, 1).at[top], at_x(1))
    left_top.wait_recv()
    right_bottom.wait_recv()
    left_bottom.wait_recv()
    across_bottom = send(chan_slot(3, 1).at[bottom], chan_slot(2, 1).at[bottom], at_x(-1))
    sent += [across_top, across_bottom]
    far_top.wait_recv()
    far_bottom.wait_recv()
    across_top.wait_recv()
    across_bottom.wait_recv()

    mine_at = partners[0, ci]
    theirs_at = partners[0, chan_id(x, yh, 1 - core)]

    def slot_of(block):
        dx = (x - block // 4 + NX) % NX
        dy = (yh + (block // 2) % 2) % 2
        return 2 * dx + dy

    sis_send[...] = chan_got[slot_of(theirs_at)]
    swap = send(sis_send, sis_recv, sister)
    sent.append(swap)
    swap.wait_recv()
    keep = jnp.where(mine_at % 2 == core, 1.0, 0.0)
    other = 1.0 - keep
    mine_slot = slot_of(mine_at)

    shift = (CH - JS * z) % CH
    group_of = lax.broadcasted_iota(jnp.int32, (24, CH), 1) // JS

    def chosen(row):
        picked = to_f32(chan_got[mine_slot, row : row + 48]) * keep
        picked = picked + to_f32(sis_recv[row : row + 48]) * other
        return pltpu.roll(picked, shift, 1)

    for i in range(NBIN // 2):
        coded[48 * i : 48 * i + 48] = chosen(48 * i)
    powers = to_f32(chan_got[mine_slot, ROWS : ROWS + 32]) * keep
    powers = powers + to_f32(sis_recv[ROWS : ROWS + 32]) * other
    coded[ROWS : ROWS + 32] = pltpu.roll(powers, shift, 1)

    def pack(d, carry):
        for r in range(0, PIECE, 24):
            piece = jnp.zeros((24, CH), jnp.float32)
            for g in range(NZ):
                row = GROUP * g + r if r < GROUP else ROWS
                moved = pltpu.roll(coded[row : row + 24], (JS * (g - d) + CH) % CH, 1)
                piece = jnp.where(group_of == g, moved, piece)
            turned[d, r : r + 24] = piece
        piece_send[d] = to_i16(turned[d])
        return carry

    lax.fori_loop(0, NZ, pack, 0)
    pieces = [send(piece_send.at[d], piece_got.at[d], at_z(d)) for d in range(1, NZ)]
    sent += pieces

    right.wait_recv()
    left.wait_recv()
    unpack_a(4, z_got, 4)

    row_of = lax.broadcasted_iota(jnp.int32, (24, CH), 0)
    sign = jnp.where(row_of < LWIN, -1.0, 1.0)
    for copy in pieces:
        copy.wait_recv()
    for d in range(NZ):
        codes = to_f32((piece_send if d == 0 else piece_got)[d])
        scale = jnp.exp2(codes[GROUP:]) * (1.0 / 32767.0)
        for k in range(3):
            value = codes[24 * k : 24 * k + 24] * scale
            flat[2 * k, 24 * d : 24 * d + 24] = value
            flat[2 * k + 1, 24 * d : 24 * d + 24] = pltpu.roll(value, LWIN, 0) * sign
    for k in range(3):
        for part in range(2):
            high, low = split(flat[2 * k + part].T)
            e_op[k, part] = high
            e_op[k, 2 + part] = low

    row8 = lax.broadcasted_iota(jnp.int32, (8, CH), 0)

    def bins(g, carry):
        rows = pl.ds(pl.multiple_of(JS * g, JS), JS)
        for k in range(3):
            f = 3 * g + k
            high, low = split(a_val[f])
            left_op = jnp.concatenate([e_op[k, n, rows] for n in range(4)], axis=0)
            got = jnp.dot(
                left_op, jnp.concatenate([high, low], axis=1), preferred_element_type=jnp.float32
            )
            got = got[:, :CH] + got[:, CH:]
            got = got[: 2 * JS] + got[2 * JS :]
            for n in range(2):
                re, im = got[8 * n : 8 * n + 8], got[JS + 8 * n : JS + 8 * n + 8]
                part_sum[2 * n, f] = jnp.where(row8 < 4, re, pltpu.roll(im, 4, 0))
                part_sum[2 * n + 1, f] = jnp.where(row8 < 4, pltpu.roll(re, 4, 0), im)
        return carry

    lax.fori_loop(0, NZ, bins, 0)
    sums = [
        send(part_sum.at[(yl + e) % NYL], part_got.at[e - 1], at_yl(e)) for e in range(1, NYL)
    ]
    sent += sums
    for copy in sums:
        copy.wait_recv()
    norm = 1.0 / math.sqrt(LWIN * NTM)
    total = (part_sum[yl] + part_got[0]) + (part_got[1] + part_got[2])
    flat[0] = (total * norm).reshape(KDIM, CH)
    for j in range(4):
        for part in range(2):
            rows = flat[0, pl.ds(4 * part + j, NBIN, stride=8), :]
            at = 24 * (2 * j + part)
            flat[1, at : at + 24] = rows
    out_ref[0] = flat[1].T
    for copy in sent:
        copy.wait_send()


def shards(records, fir_taps, partners):
    taps = fir_taps.astype(jnp.float32)
    line = jnp.concatenate([taps[256:], jnp.zeros((255,), jnp.float32), taps[:256]])
    line = line.reshape(1, 512)
    f32, bf16, i16 = jnp.float32, jnp.bfloat16, jnp.int16
    vmem = pltpu.VMEM
    copies = 2 + 2 + 4 + 8 + 2 + 4 + 2 + 1 + 7 + 3 + 4
    return pl.pallas_call(
        kernel,
        out_shape=jax.ShapeDtypeStruct((1, CH, KDIM), f32),
        in_specs=[
            pl.BlockSpec(memory_space=pltpu.SMEM),
            pl.BlockSpec(memory_space=pltpu.VMEM),
            pl.BlockSpec(memory_space=pl.ANY),
            pl.BlockSpec(memory_space=pl.ANY),
        ],
        out_specs=pl.BlockSpec(memory_space=pltpu.VMEM),
        scratch_shapes=[
            vmem((CH, LWIN * HOP), bf16),
            vmem((2 * NQ, WIN + 4 * HALF), bf16),
            vmem((4 * NQ, HOP), bf16),
            vmem((2 * NQ, 128), bf16),
            vmem((2 * NQ, 128), bf16),
            vmem((16, NQ, CH), f32),
            vmem((2, NQ, CH), f32),
            vmem((NQ, CH), f32),
            vmem((2, NQ, CH), f32),
            vmem((NQ, CH), f32),
            vmem((SPEC, CH), f32),
            vmem((8, SPEC, CH), i16),
            vmem((NZ, SPEC, CH), i16),
            vmem((NBIN, KDIM, CH), f32),
            vmem((SPEC, CH), i16),
            vmem((SPEC, CH), i16),
            vmem((NZ, PIECE, CH), i16),
            vmem((NZ, PIECE, CH), i16),
            vmem((3, 4, CH, KDIM), bf16),
            vmem((NYL, NBIN, 8, CH), f32),
            vmem((NYL - 1, NBIN, 8, CH), f32),
            vmem((6, KDIM, CH), f32),
            vmem((NZ, PIECE, CH), f32),
            pltpu.SemaphoreType.DMA((6,)),
            pltpu.SemaphoreType.DMA,
            pltpu.SemaphoreType.DMA((copies,)),
            pltpu.SemaphoreType.DMA((copies,)),
        ],
        compiler_params=pltpu.CompilerParams(collective_id=0, has_side_effects=True),
    )(partners, line, jnp.asarray(basis_table()), records)


def solution(mesh):
    placed = (P("chan", "tm"), P(), P())
    return jax.shard_map(
        shards, mesh=mesh, in_specs=placed, out_specs=P(None, "chan", "tm"), check_vma=False
    )
```

```python
import functools
import math

import jax
import jax.numpy as jnp
import ml_dtypes
import numpy as np
from jax import lax
from jax.experimental import pallas as pl
from jax.experimental.pallas import tpu as pltpu
from jax.sharding import PartitionSpec as P

WIN = 2560
HOP = WIN // 2
NBIN = 24
HALF = 128
FIRST_BIN = 4
NQ = 2 * NBIN
CH = 128
LWIN = 12
SPEC = 608
NX, NYH, NC = 4, 2, 2
NZ, NYL = 8, 4
NTM = NZ * NYL
JS = CH // NZ
PIECE = 96
KDIM = NZ * 2 * LWIN
COUNTS = (8, 4)
BASES = (0, 400)
CHUNKS = (pl.ds(0, 400), pl.ds(400, 208))
HEAD, TAIL = pl.ds(0, 304), pl.ds(304, 96)
BLOCKS = ((0, 80), (80, 80), (160, 80), (240, 80), (320, 80), (400, 112), (512, 96))
MESH = pl.DeviceIdType.MESH
NT = (((1,), (1,)), ((), ()))


def basis_table():
    t = np.arange(WIN)
    edge = np.minimum(t, WIN - 1 - t)
    ramp = np.sin(math.pi * (edge + 0.5) / (2.0 * HALF))
    taper = np.where(edge < HALF, ramp * ramp, 1.0) / math.sqrt(WIN)
    phase = (np.arange(NBIN)[:, None] + FIRST_BIN) * t[None, :] % WIN
    angle = 2.0 * math.pi / WIN * phase
    table = np.concatenate([np.cos(angle), -np.sin(angle)], axis=0) * taper
    table = np.pad(table, ((0, 0), (2 * HALF, 2 * HALF))).astype(np.float32)
    high = table.astype(ml_dtypes.bfloat16)
    low = (table - high.astype(np.float32)).astype(ml_dtypes.bfloat16)
    return np.concatenate([high, low], axis=0)


def split(value):
    high = value.astype(jnp.bfloat16)
    return high, (value - high.astype(jnp.float32)).astype(jnp.bfloat16)


def to_f32(codes):
    return codes.astype(jnp.int32).astype(jnp.float32)


def to_i16(value):
    return value.astype(jnp.int32).astype(jnp.int16)


def kernel(
    partners, taps, basis_hbm, x_hbm, out_ref,
    xs, basis, d_op, e_first, e_last, acc, up_send, low_send, up_recv, low_recv,
    coded, chan_a, chan_b, z_got, a_val, sis_send, sis_recv, piece_send, piece_got,
    e_op, part_sum, part_got, flat, turned, line,
    x_sem, basis_sem, send_sem, recv_sem,
):
    ci, ti = lax.axis_index("chan"), lax.axis_index("tm")
    x, yh, core = ci // 4, (ci // 2) % 2, ci % 2
    z, yl = ti // NYL, ti % NYL

    def chan_id(xx, yy, cc):
        return (xx * 2 + yy) * 2 + cc

    def at_x(step):
        return (chan_id((x + step + NX) % NX, yh, core), ti)

    def at_z(step):
        return (ci, ((z + step + NZ) % NZ) * NYL + yl)

    def at_yl(step):
        return (ci, z * NYL + (yl + step) % NYL)

    def at_tm(step):
        return (ci, (ti + step + NTM) % NTM)

    across = (chan_id(x, 1 - yh, core), ti)
    sister = (chan_id(x, yh, 1 - core), ti)

    fetch_basis = pltpu.make_async_copy(basis_hbm, basis, basis_sem)
    fetch_basis.start()
    pair_order = [0, 5, 1, 2, 3, 4]

    def fetch(p):
        cols = pl.ds(2 * HOP * p, 2 * HOP)
        return pltpu.make_async_copy(x_hbm.at[:, cols], xs.at[:, cols], x_sem.at[p])

    for p in pair_order:
        fetch(p).start()

    barrier = pltpu.get_barrier_semaphore()
    peers = [at_tm(1), at_tm(-1), across, sister, at_x(1), at_x(-1)]
    peers += [at_z(d) for d in range(1, NZ)] + [at_yl(e) for e in range(1, NYL)]
    for peer in peers:
        pl.semaphore_signal(barrier, inc=1, device_id=peer, device_id_type=MESH)

    counter = [0]

    def send(src, dst, device):
        slot = counter[0]
        counter[0] += 1
        copy = pltpu.make_async_remote_copy(
            src_ref=src, dst_ref=dst, send_sem=send_sem.at[slot], recv_sem=recv_sem.at[slot],
            device_id=device, device_id_type=MESH,
        )
        copy.start()
        sent.append(copy)
        return copy

    sent = []

    acc[...] = jnp.zeros_like(acc)
    row = taps[...].astype(jnp.float32).reshape(1, 257)
    line[...] = jnp.zeros_like(line)
    line[:, 256:] = row[:, :256]
    line[:, :1] = row[:, 256:]
    toep = pltpu.roll(jnp.broadcast_to(line[...], (512, 512)), 0, 1, stride=1, stride_axis=0)
    toep = toep[:, :256].astype(jnp.bfloat16)
    fetch_basis.wait()
    for i in range(11):
        both = jnp.dot(
            basis[:, 256 * i : 256 * i + 512], toep, preferred_element_type=jnp.float32
        )
        high, low = split(both[:NQ] + both[NQ:])
        for half in range(2):
            j = 2 * i + half
            h_part = high[:, 128 * half : 128 * half + 128]
            l_part = low[:, 128 * half : 128 * half + 128]
            if j == 0:
                e_last[:NQ, :] = h_part
                e_last[NQ:, :] = l_part
            elif j == 21:
                e_first[:NQ, :] = h_part
                e_first[NQ:, :] = l_part
            else:
                row = 0 if j <= 10 else 2 * NQ
                col = 128 * ((j - 1) % 10)
                d_op[row : row + NQ, col : col + 128] = h_part
                d_op[row + NQ : row + 2 * NQ, col : col + 128] = l_part

    def hop_pair(p):
        fetch(p).wait()
        base = pl.multiple_of(2 * HOP * p, 128)
        second = pl.multiple_of(2 * HOP * p + HOP, 128)
        tail_a = pl.multiple_of(2 * HOP * p + HOP - 128, 128)
        tail_b = pl.multiple_of(2 * HOP * p + 2 * HOP - 128, 128)

        def both_hops(first, other, width):
            return jnp.concatenate([xs[:, pl.ds(first, width)], xs[:, pl.ds(other, width)]], axis=0)

        def product(left, right):
            return lax.dot_general(left, right, NT, preferred_element_type=jnp.float32)

        main = product(d_op[...], both_hops(base, second, HOP))
        first = product(e_first[...], both_hops(base, second, 128))
        last = product(e_last[...], both_hops(tail_a, tail_b, 128))
        p0 = main[:NQ] + main[NQ : 2 * NQ]
        p1 = main[2 * NQ : 3 * NQ] + main[3 * NQ :]
        p2 = first[:NQ] + first[NQ:]
        p3 = last[:NQ] + last[NQ:]
        for hop in range(2):
            lanes = slice(128 * hop, 128 * hop + 128)
            at = 2 * p + hop
            acc[at] += p2[:, lanes]
            acc[at + 1] += p1[:, lanes]
            acc[at + 2] += p0[:, lanes]
            acc[at + 3] += p3[:, lanes]

    hop_pair(0)
    hop_pair(5)
    up_send[...] = acc[0:2]
    low_send[...] = acc[14]
    pl.semaphore_wait(barrier, len(peers))
    up = send(up_send, up_recv, at_tm(-1))
    low = send(low_send, low_recv, at_tm(1))
    pl.loop(1, 5)(hop_pair)

    limit = jnp.float32(32767.0)

    def whiten(w, chunk, i):
        base, n = BASES[chunk], COUNTS[chunk]
        spec = acc[w + 2]
        real, imag = spec[:NBIN], spec[NBIN:]
        amp = jnp.sqrt(real * real + imag * imag + 1.0)
        real, imag = real / amp, imag / amp
        top = jnp.max(jnp.maximum(jnp.abs(real), jnp.abs(imag)), axis=0, keepdims=True)
        power = jnp.ceil(jnp.log2(jnp.maximum(top, 1e-30)))
        gain = limit / jnp.exp2(power)
        for part, value in enumerate((real, imag)):
            code = jnp.clip(jnp.floor(value * gain + 0.5), -limit, limit)
            coded[pl.ds(base + part * n + i, NBIN, stride=2 * n), :] = code
            at = base + NQ * n + part * n + i
            coded[at : at + 1, :] = power

    chan_got = (chan_a, chan_b)

    def chan_slot(dx, dy, chunk):
        return chan_got[chunk].at[2 * dx + dy]

    def launch(chunk):
        rows = CHUNKS[chunk]
        own = chan_slot(0, 0, chunk)
        return [
            send(own, chan_slot(0, 1, chunk), across),
            send(own, z_got.at[1, rows], at_z(1)),
            send(own, z_got.at[7, rows], at_z(-1)),
            send(own, chan_slot(1, 0, chunk), at_x(1)),
            send(own, chan_slot(3, 0, chunk), at_x(-1)),
        ]

    for i in range(8):
        whiten(i + 1, 0, i)
    for r, size in BLOCKS[:5]:
        chan_a[0, r : r + size] = to_i16(coded[r : r + size])
    first = launch(0)
    coded[600:, :] = jnp.zeros((8, CH), jnp.float32)
    whiten(9, 1, 1)
    low.wait_recv()
    acc[2] += jnp.where(ti > 0, 1.0, 0.0) * low_recv[...]
    whiten(0, 1, 0)
    up.wait_recv()
    acc[12:14] += jnp.where(ti < NTM - 1, 1.0, 0.0) * up_recv[...]
    whiten(10, 1, 2)
    whiten(11, 1, 3)
    for r, size in BLOCKS[5:]:
        chan_b[0, r - 400 : r - 400 + size] = to_i16(coded[r : r + size])
    second = launch(1)
    own_sent = (first, second)

    def unpack_a(d, source, index, chunk, base=None):
        base, n = BASES[chunk] if base is None else base, COUNTS[chunk]
        at = 24 * d + 16 * chunk
        power = to_f32(source[index, base + NQ * n : base + NQ * n + 16])
        scale = jnp.exp2(power[: 2 * n]) * (1.0 / 32767.0)
        for i in range(n // 2 * 6):
            block = to_f32(source[index, base + 16 * i : base + 16 * i + 16])
            for k in range(8 // n):
                f = i * (8 // n) + k
                a_val[f, at : at + 2 * n] = block[2 * n * k : 2 * n * k + 2 * n] * scale

    def ring(step, chunk, right, left):
        right.wait_recv()
        left.wait_recv()
        rows = CHUNKS[chunk]
        right = send(z_got.at[step, rows], z_got.at[step + 1, rows], at_z(1))
        left = send(z_got.at[8 - step, rows], z_got.at[7 - step, rows], at_z(-1))
        return right, left

    def far_z(chunk):
        if chunk == 0:
            return [
                send(z_got.at[3, HEAD], z_got.at[4, HEAD], at_z(1)),
                send(z_got.at[5, TAIL], z_got.at[4, TAIL], at_z(-1)),
            ]
        rows = CHUNKS[1]
        return [send(z_got.at[5, rows], z_got.at[4, rows], at_z(-1))]

    def far_x(dy, chunk):
        before, after, target = [chan_slot(dx, dy, chunk) for dx in (1, 3, 2)]
        if chunk == 0:
            return [
                send(before.at[HEAD], target.at[HEAD], at_x(1)),
                send(after.at[TAIL], target.at[TAIL], at_x(-1)),
            ]
        return [send(after, target, at_x(-1))]

    zr, zl = [None, None], [None, None]
    far_own = []
    for c in range(2):
        zr[c], zl[c] = ring(1, c, own_sent[c][1], own_sent[c][2])
        own_sent[c][3].wait_recv()
        own_sent[c][4].wait_recv()
        far_own += far_x(0, c)
        unpack_a(0, chan_got[c], 0, c, 0)
    by_x = []
    for c in range(2):
        own_sent[c][0].wait_recv()
        by_x.append((
            send(chan_slot(0, 1, c), chan_slot(1, 1, c), at_x(1)),
            send(chan_slot(0, 1, c), chan_slot(3, 1, c), at_x(-1)),
        ))
        unpack_a(1, z_got, 1, c)
        unpack_a(7, z_got, 7, c)
        zr[c], zl[c] = ring(2, c, zr[c], zl[c])
    far_next = []
    for c in range(2):
        by_x[c][0].wait_recv()
        by_x[c][1].wait_recv()
        far_next.append(far_x(1, c))
        unpack_a(2, z_got, 2, c)
        unpack_a(6, z_got, 6, c)
    zr[0].wait_recv()
    zl[0].wait_recv()
    last = far_z(0)
    for copy in far_own:
        copy.wait_recv()

    mine_at = partners[0, ci]
    theirs_at = partners[0, chan_id(x, yh, 1 - core)]

    def slot_of(block):
        dx = (x - block // 4 + NX) % NX
        dy = (yh + (block // 2) % 2) % 2
        return 2 * dx + dy

    theirs_slot = slot_of(theirs_at)
    swaps = []
    for c in range(2):
        rows = CHUNKS[c]
        for copy in far_next[c]:
            copy.wait_recv()
        for r, size in BLOCKS[:5] if c == 0 else BLOCKS[5:]:
            at = r - BASES[c]
            sis_send[r : r + size] = chan_got[c][theirs_slot, at : at + size]
        swaps.append(send(sis_send.at[rows], sis_recv.at[rows], sister))
        if c == 0:
            zr[1].wait_recv()
            zl[1].wait_recv()
            last += far_z(1)
    keep = jnp.where(mine_at % 2 == core, 1.0, 0.0)
    other = 1.0 - keep
    mine_slot = slot_of(mine_at)
    shift = (CH - JS * z) % CH

    def pack(d, chunk):
        base, n = BASES[chunk], COUNTS[chunk]
        for r in range(0, 8 * n, 2 * n):
            piece = jnp.zeros((2 * n, CH), jnp.float32)
            group_of = lax.broadcasted_iota(jnp.int32, (2 * n, CH), 1) // JS
            for g in range(NZ):
                row = base + (6 * n * g + r if r < 6 * n else NQ * n)
                moved = coded[row : row + 2 * n]
                if g != d:
                    moved = pltpu.roll(moved, (JS * (g - d) + CH) % CH, 1)
                piece = jnp.where(group_of == g, moved, piece)
            at = 64 * chunk + r
            turned[d, at : at + 2 * n] = piece
        rows = pl.ds(64 * chunk, 8 * n)
        piece_send[d, rows] = to_i16(turned[d, rows])

    pieces = []
    for c in range(2):
        swaps[c].wait_recv()
        for r, size in BLOCKS[:5] if c == 0 else BLOCKS[5:]:
            at = r - BASES[c]
            picked = to_f32(chan_got[c][mine_slot, at : at + size]) * keep
            picked = picked + to_f32(sis_recv[r : r + size]) * other
            coded[r : r + size] = pltpu.roll(picked, shift, 1)
        rows = pl.ds(64 * c, 8 * COUNTS[c])
        batch = []
        for d in (4, 3, 5, 2, 6, 1, 7):
            pack(d, c)
            batch.append((d, send(piece_send.at[d, rows], piece_got.at[d, rows], at_z(d))))
        pack(0, c)
        pieces.append(batch)
    for c in range(2):
        unpack_a(3, z_got, 3, c)
        unpack_a(5, z_got, 5, c)
    for copy in last:
        copy.wait_recv()
    unpack_a(4, z_got, 4, 0)
    unpack_a(4, z_got, 4, 1)

    sign = jnp.where(lax.broadcasted_iota(jnp.int32, (8, CH), 0) < 4, -1.0, 1.0)

    def unpack_e(d, source, chunk):
        n = COUNTS[chunk]
        codes = to_f32(source[d, pl.ds(64 * chunk, 8 * n)])
        scale = jnp.exp2(codes[6 * n :]) * (1.0 / 32767.0)
        at = 24 * d + 16 * chunk
        for k in range(3):
            value = codes[2 * n * k : 2 * n * k + 2 * n] * scale
            flat[2 * k, at : at + 2 * n] = value
            if chunk == 0:
                flat[2 * k + 1, at : at + 8] = -value[8:]
                flat[2 * k + 1, at + 8 : at + 16] = value[:8]
            else:
                flat[2 * k + 1, at : at + 8] = pltpu.roll(value, 4, 0) * sign

    for c in range(2):
        unpack_e(0, piece_send, c)
        for d, copy in pieces[c][::-1]:
            copy.wait_recv()
            unpack_e(d, piece_got, c)
    for k in range(3):
        for part in range(2):
            high, low = split(flat[2 * k + part].T)
            e_op[k, part] = high
            e_op[k, 2 + part] = low

    row8 = lax.broadcasted_iota(jnp.int32, (8, CH), 0)

    def bins(g, carry):
        rows = pl.ds(pl.multiple_of(JS * g, JS), JS)
        for k in range(3):
            f = 3 * g + k
            high, low = split(a_val[f])
            left_op = jnp.concatenate([e_op[k, n, rows] for n in range(4)], axis=0)
            got = jnp.dot(
                left_op, jnp.concatenate([high, low], axis=1), preferred_element_type=jnp.float32
            )
            got = got[:, :CH] + got[:, CH:]
            got = got[: 2 * JS] + got[2 * JS :]
            for n in range(2):
                re, im = got[8 * n : 8 * n + 8], got[JS + 8 * n : JS + 8 * n + 8]
                part_sum[2 * n, f] = jnp.where(row8 < 4, re, pltpu.roll(im, 4, 0))
                part_sum[2 * n + 1, f] = jnp.where(row8 < 4, pltpu.roll(re, 4, 0), im)
        return carry

    sums = []
    for h in range(2):
        lax.fori_loop(4 * h, 4 * h + 4, bins, 0)
        bin_rows = pl.ds(12 * h, 12)
        for e in (2, 1, 3):
            target = (yl + e) % NYL
            sums.append(
                send(part_sum.at[target, bin_rows], part_got.at[e - 1, bin_rows], at_yl(e))
            )
    for copy in sums:
        copy.wait_recv()
    norm = 1.0 / math.sqrt(LWIN * NTM)
    total = (part_sum[yl] + part_got[0]) + (part_got[1] + part_got[2])
    flat[0] = (total * norm).reshape(KDIM, CH)
    for j in range(4):
        for part in range(2):
            rows = flat[0, pl.ds(4 * part + j, NBIN, stride=8), :]
            at = 24 * (2 * j + part)
            flat[1, at : at + 24] = rows
    out_ref[0] = flat[1].T
    for copy in sent:
        copy.wait_send()


def shards(records, fir_taps, partners):
    f32, bf16, i16 = jnp.float32, jnp.bfloat16, jnp.int16
    vmem = pltpu.VMEM
    copies = 55
    return pl.pallas_call(
        kernel,
        out_shape=jax.ShapeDtypeStruct((1, CH, KDIM), f32),
        in_specs=[
            pl.BlockSpec(memory_space=pltpu.SMEM),
            pl.BlockSpec(memory_space=pltpu.VMEM),
            pl.BlockSpec(memory_space=pl.ANY),
            pl.BlockSpec(memory_space=pl.ANY),
        ],
        out_specs=pl.BlockSpec(memory_space=pltpu.VMEM),
        scratch_shapes=[
            vmem((CH, LWIN * HOP), bf16),
            vmem((2 * NQ, WIN + 4 * HALF), bf16),
            vmem((4 * NQ, HOP), bf16),
            vmem((2 * NQ, 128), bf16),
            vmem((2 * NQ, 128), bf16),
            vmem((16, NQ, CH), f32),
            vmem((2, NQ, CH), f32),
            vmem((NQ, CH), f32),
            vmem((2, NQ, CH), f32),
            vmem((NQ, CH), f32),
            vmem((SPEC, CH), f32),
            vmem((8, 400, CH), i16),
            vmem((8, 208, CH), i16),
            vmem((NZ, SPEC, CH), i16),
            vmem((NBIN, KDIM, CH), f32),
            vmem((SPEC, CH), i16),
            vmem((SPEC, CH), i16),
            vmem((NZ, PIECE, CH), i16),
            vmem((NZ, PIECE, CH), i16),
            vmem((3, 4, CH, KDIM), bf16),
            vmem((NYL, NBIN, 8, CH), f32),
            vmem((NYL - 1, NBIN, 8, CH), f32),
            vmem((6, KDIM, CH), f32),
            vmem((NZ, PIECE, CH), f32),
            vmem((1, 512), f32),
            pltpu.SemaphoreType.DMA((6,)),
            pltpu.SemaphoreType.DMA,
            pltpu.SemaphoreType.DMA((copies,)),
            pltpu.SemaphoreType.DMA((copies,)),
        ],
        compiler_params=pltpu.CompilerParams(collective_id=0, has_side_effects=True),
    )(partners, fir_taps, jnp.asarray(basis_table()), records)


def solution(mesh):
    placed = (P("chan", "tm"), P(), P())
    return jax.shard_map(
        shards, mesh=mesh, in_specs=placed, out_specs=P(None, "chan", "tm"), check_vma=False
    )
```

```python
import functools
import math

import jax
import jax.numpy as jnp
import ml_dtypes
import numpy as np
from jax import lax
from jax.experimental import pallas as pl
from jax.experimental.pallas import tpu as pltpu
from jax.sharding import PartitionSpec as P

WIN = 2560
HOP = WIN // 2
NBIN = 24
HALF = 128
FIRST_BIN = 4
NQ = 2 * NBIN
CH = 128
LWIN = 12
SPEC = 608
NX, NYH, NC = 4, 2, 2
NZ, NYL = 8, 4
NTM = NZ * NYL
JS = CH // NZ
PIECE = 96
KDIM = NZ * 2 * LWIN
COUNTS = (8, 4)
BASES = (0, 400)
CHUNKS = (pl.ds(0, 400), pl.ds(400, 208))
HEAD, TAIL = pl.ds(0, 304), pl.ds(304, 96)
BLOCKS = ((0, 80), (80, 80), (160, 80), (240, 80), (320, 80), (400, 112), (512, 96))
MESH = pl.DeviceIdType.MESH
NT = (((1,), (1,)), ((), ()))


def basis_table():
    t = np.arange(WIN)
    edge = np.minimum(t, WIN - 1 - t)
    ramp = np.sin(math.pi * (edge + 0.5) / (2.0 * HALF))
    taper = np.where(edge < HALF, ramp * ramp, 1.0) / math.sqrt(WIN)
    phase = (np.arange(NBIN)[:, None] + FIRST_BIN) * t[None, :] % WIN
    angle = 2.0 * math.pi / WIN * phase
    table = np.concatenate([np.cos(angle), -np.sin(angle)], axis=0) * taper
    table = np.pad(table, ((0, 0), (2 * HALF, 2 * HALF))).astype(np.float32)
    high = table.astype(ml_dtypes.bfloat16)
    low = (table - high.astype(np.float32)).astype(ml_dtypes.bfloat16)
    return np.concatenate([high, low], axis=0)


def split(value):
    high = value.astype(jnp.bfloat16)
    return high, (value - high.astype(jnp.float32)).astype(jnp.bfloat16)


def to_f32(codes):
    return codes.astype(jnp.int32).astype(jnp.float32)


def to_i16(value):
    return value.astype(jnp.int32).astype(jnp.int16)


def kernel(
    partners, taps, basis_hbm, x_hbm, out_ref,
    xs, basis, d_op, e_first, e_last, acc, up_send, low_send, up_recv, low_recv,
    coded, chan_a, chan_b, z_got, a_val, sis_send, sis_recv, piece_send, piece_got,
    e_op, part_val, part_code, part_got, flat, turned, line,
    x_sem, basis_sem, send_sem, recv_sem,
):
    ci, ti = lax.axis_index("chan"), lax.axis_index("tm")
    x, yh, core = ci // 4, (ci // 2) % 2, ci % 2
    z, yl = ti // NYL, ti % NYL

    def chan_id(xx, yy, cc):
        return (xx * 2 + yy) * 2 + cc

    def at_x(step):
        return (chan_id((x + step + NX) % NX, yh, core), ti)

    def at_z(step):
        return (ci, ((z + step + NZ) % NZ) * NYL + yl)

    def at_yl(step):
        return (ci, z * NYL + (yl + step) % NYL)

    def at_tm(step):
        return (ci, (ti + step + NTM) % NTM)

    across = (chan_id(x, 1 - yh, core), ti)
    sister = (chan_id(x, yh, 1 - core), ti)

    fetch_basis = pltpu.make_async_copy(basis_hbm, basis, basis_sem)
    fetch_basis.start()
    pair_order = [0, 5, 1, 2, 3, 4]

    def fetch(p):
        cols = pl.ds(2 * HOP * p, 2 * HOP)
        return pltpu.make_async_copy(x_hbm.at[:, cols], xs.at[:, cols], x_sem.at[p])

    for p in pair_order:
        fetch(p).start()

    barrier = pltpu.get_barrier_semaphore()
    peers = [at_tm(1), at_tm(-1), across, sister, at_x(1), at_x(-1)]
    peers += [at_z(d) for d in range(1, NZ)] + [at_yl(e) for e in range(1, NYL)]
    for peer in peers:
        pl.semaphore_signal(barrier, inc=1, device_id=peer, device_id_type=MESH)

    counter = [0]

    def send(src, dst, device):
        slot = counter[0]
        counter[0] += 1
        copy = pltpu.make_async_remote_copy(
            src_ref=src, dst_ref=dst, send_sem=send_sem.at[slot], recv_sem=recv_sem.at[slot],
            device_id=device, device_id_type=MESH,
        )
        copy.start()
        sent.append(copy)
        return copy

    sent = []

    acc[...] = jnp.zeros_like(acc)
    row = taps[...].astype(jnp.float32).reshape(1, 257)
    line[...] = jnp.zeros_like(line)
    line[:, 256:] = row[:, :256]
    line[:, :1] = row[:, 256:]
    toep = pltpu.roll(jnp.broadcast_to(line[...], (512, 512)), 0, 1, stride=1, stride_axis=0)
    toep = toep[:, :256].astype(jnp.bfloat16)
    fetch_basis.wait()
    for i in range(11):
        both = jnp.dot(
            basis[:, 256 * i : 256 * i + 512], toep, preferred_element_type=jnp.float32
        )
        high, low = split(both[:NQ] + both[NQ:])
        for half in range(2):
            j = 2 * i + half
            h_part = high[:, 128 * half : 128 * half + 128]
            l_part = low[:, 128 * half : 128 * half + 128]
            if j == 0:
                e_last[:NQ, :] = h_part
                e_last[NQ:, :] = l_part
            elif j == 21:
                e_first[:NQ, :] = h_part
                e_first[NQ:, :] = l_part
            else:
                row = 0 if j <= 10 else 2 * NQ
                col = 128 * ((j - 1) % 10)
                d_op[row : row + NQ, col : col + 128] = h_part
                d_op[row + NQ : row + 2 * NQ, col : col + 128] = l_part

    def hop_pair(p):
        fetch(p).wait()
        base = pl.multiple_of(2 * HOP * p, 128)
        second = pl.multiple_of(2 * HOP * p + HOP, 128)
        tail_a = pl.multiple_of(2 * HOP * p + HOP - 128, 128)
        tail_b = pl.multiple_of(2 * HOP * p + 2 * HOP - 128, 128)

        def both_hops(first, other, width):
            return jnp.concatenate([xs[:, pl.ds(first, width)], xs[:, pl.ds(other, width)]], axis=0)

        def product(left, right):
            return lax.dot_general(left, right, NT, preferred_element_type=jnp.float32)

        main = product(d_op[...], both_hops(base, second, HOP))
        first = product(e_first[...], both_hops(base, second, 128))
        last = product(e_last[...], both_hops(tail_a, tail_b, 128))
        p0 = main[:NQ] + main[NQ : 2 * NQ]
        p1 = main[2 * NQ : 3 * NQ] + main[3 * NQ :]
        p2 = first[:NQ] + first[NQ:]
        p3 = last[:NQ] + last[NQ:]
        for hop in range(2):
            lanes = slice(128 * hop, 128 * hop + 128)
            at = 2 * p + hop
            acc[at] += p2[:, lanes]
            acc[at + 1] += p1[:, lanes]
            acc[at + 2] += p0[:, lanes]
            acc[at + 3] += p3[:, lanes]

    hop_pair(0)
    hop_pair(5)
    up_send[...] = acc[0:2]
    low_send[...] = acc[14]
    pl.semaphore_wait(barrier, len(peers))
    up = send(up_send, up_recv, at_tm(-1))
    low = send(low_send, low_recv, at_tm(1))
    pl.loop(1, 5)(hop_pair)

    limit = jnp.float32(32767.0)

    def whiten(w, chunk, i):
        base, n = BASES[chunk], COUNTS[chunk]
        spec = acc[w + 2]
        real, imag = spec[:NBIN], spec[NBIN:]
        amp = jnp.sqrt(real * real + imag * imag + 1.0)
        real, imag = real / amp, imag / amp
        top = jnp.max(jnp.maximum(jnp.abs(real), jnp.abs(imag)), axis=0, keepdims=True)
        power = jnp.ceil(jnp.log2(jnp.maximum(top, 1e-30)))
        gain = limit / jnp.exp2(power)
        for part, value in enumerate((real, imag)):
            code = jnp.clip(jnp.floor(value * gain + 0.5), -limit, limit)
            coded[pl.ds(base + part * n + i, NBIN, stride=2 * n), :] = code
            at = base + NQ * n + part * n + i
            coded[at : at + 1, :] = power

    chan_got = (chan_a, chan_b)

    def chan_slot(dx, dy, chunk):
        return chan_got[chunk].at[2 * dx + dy]

    def launch(chunk):
        rows = CHUNKS[chunk]
        own = chan_slot(0, 0, chunk)
        return [
            send(own, chan_slot(0, 1, chunk), across),
            send(own, z_got.at[1, rows], at_z(1)),
            send(own, z_got.at[7, rows], at_z(-1)),
            send(own, chan_slot(1, 0, chunk), at_x(1)),
            send(own, chan_slot(3, 0, chunk), at_x(-1)),
        ]

    for i in range(8):
        whiten(i + 1, 0, i)
    for r, size in BLOCKS[:5]:
        chan_a[0, r : r + size] = to_i16(coded[r : r + size])
    first = launch(0)
    coded[600:, :] = jnp.zeros((8, CH), jnp.float32)
    whiten(9, 1, 1)
    low.wait_recv()
    acc[2] += jnp.where(ti > 0, 1.0, 0.0) * low_recv[...]
    whiten(0, 1, 0)
    up.wait_recv()
    acc[12:14] += jnp.where(ti < NTM - 1, 1.0, 0.0) * up_recv[...]
    whiten(10, 1, 2)
    whiten(11, 1, 3)
    for r, size in BLOCKS[5:]:
        chan_b[0, r - 400 : r - 400 + size] = to_i16(coded[r : r + size])
    second = launch(1)
    own_sent = (first, second)

    def unpack_a(d, source, index, chunk, base=None):
        base, n = BASES[chunk] if base is None else base, COUNTS[chunk]
        at = 24 * d + 16 * chunk
        power = to_f32(source[index, base + NQ * n : base + NQ * n + 16])
        scale = jnp.exp2(power[: 2 * n]) * (1.0 / 32767.0)
        for i in range(n // 2 * 6):
            block = to_f32(source[index, base + 16 * i : base + 16 * i + 16])
            for k in range(8 // n):
                f = i * (8 // n) + k
                a_val[f, at : at + 2 * n] = block[2 * n * k : 2 * n * k + 2 * n] * scale

    def ring(step, chunk, right, left):
        right.wait_recv()
        left.wait_recv()
        rows = CHUNKS[chunk]
        right = send(z_got.at[step, rows], z_got.at[step + 1, rows], at_z(1))
        left = send(z_got.at[8 - step, rows], z_got.at[7 - step, rows], at_z(-1))
        return right, left

    def far_z(chunk):
        if chunk == 0:
            return [
                send(z_got.at[3, HEAD], z_got.at[4, HEAD], at_z(1)),
                send(z_got.at[5, TAIL], z_got.at[4, TAIL], at_z(-1)),
            ]
        rows = CHUNKS[1]
        return [send(z_got.at[5, rows], z_got.at[4, rows], at_z(-1))]

    def far_x(dy, chunk):
        before, after, target = [chan_slot(dx, dy, chunk) for dx in (1, 3, 2)]
        if chunk == 0:
            return [
                send(before.at[HEAD], target.at[HEAD], at_x(1)),
                send(after.at[TAIL], target.at[TAIL], at_x(-1)),
            ]
        return [send(after, target, at_x(-1))]

    zr, zl = [None, None], [None, None]
    far_own = []
    for c in range(2):
        zr[c], zl[c] = ring(1, c, own_sent[c][1], own_sent[c][2])
        own_sent[c][3].wait_recv()
        own_sent[c][4].wait_recv()
        far_own += far_x(0, c)
        unpack_a(0, chan_got[c], 0, c, 0)
    by_x = []
    for c in range(2):
        own_sent[c][0].wait_recv()
        by_x.append((
            send(chan_slot(0, 1, c), chan_slot(1, 1, c), at_x(1)),
            send(chan_slot(0, 1, c), chan_slot(3, 1, c), at_x(-1)),
        ))
        unpack_a(1, z_got, 1, c)
        unpack_a(7, z_got, 7, c)
        zr[c], zl[c] = ring(2, c, zr[c], zl[c])
    far_next = []
    for c in range(2):
        by_x[c][0].wait_recv()
        by_x[c][1].wait_recv()
        far_next.append(far_x(1, c))
        unpack_a(2, z_got, 2, c)
        unpack_a(6, z_got, 6, c)
    zr[0].wait_recv()
    zl[0].wait_recv()
    last = far_z(0)
    for copy in far_own:
        copy.wait_recv()

    mine_at = partners[0, ci]
    theirs_at = partners[0, chan_id(x, yh, 1 - core)]

    def slot_of(block):
        dx = (x - block // 4 + NX) % NX
        dy = (yh + (block // 2) % 2) % 2
        return 2 * dx + dy

    theirs_slot = slot_of(theirs_at)
    swaps = []
    for c in range(2):
        rows = CHUNKS[c]
        for copy in far_next[c]:
            copy.wait_recv()
        for r, size in BLOCKS[:5] if c == 0 else BLOCKS[5:]:
            at = r - BASES[c]
            sis_send[r : r + size] = chan_got[c][theirs_slot, at : at + size]
        swaps.append(send(sis_send.at[rows], sis_recv.at[rows], sister))
        if c == 0:
            zr[1].wait_recv()
            zl[1].wait_recv()
            last += far_z(1)
    keep = jnp.where(mine_at % 2 == core, 1.0, 0.0)
    other = 1.0 - keep
    mine_slot = slot_of(mine_at)
    shift = (CH - JS * z) % CH

    def pack(d, chunk):
        base, n = BASES[chunk], COUNTS[chunk]
        for r in range(0, 8 * n, 2 * n):
            piece = jnp.zeros((2 * n, CH), jnp.float32)
            group_of = lax.broadcasted_iota(jnp.int32, (2 * n, CH), 1) // JS
            for g in range(NZ):
                row = base + (6 * n * g + r if r < 6 * n else NQ * n)
                moved = coded[row : row + 2 * n]
                if g != d:
                    moved = pltpu.roll(moved, (JS * (g - d) + CH) % CH, 1)
                piece = jnp.where(group_of == g, moved, piece)
            at = 64 * chunk + r
            turned[d, at : at + 2 * n] = piece
        rows = pl.ds(64 * chunk, 8 * n)
        piece_send[d, rows] = to_i16(turned[d, rows])

    pieces = []
    for c in range(2):
        swaps[c].wait_recv()
        for r, size in BLOCKS[:5] if c == 0 else BLOCKS[5:]:
            at = r - BASES[c]
            picked = to_f32(chan_got[c][mine_slot, at : at + size]) * keep
            picked = picked + to_f32(sis_recv[r : r + size]) * other
            coded[r : r + size] = pltpu.roll(picked, shift, 1)
        rows = pl.ds(64 * c, 8 * COUNTS[c])
        batch = []
        for d in (4, 3, 5, 2, 6, 1, 7):
            pack(d, c)
            batch.append((d, send(piece_send.at[d, rows], piece_got.at[d, rows], at_z(d))))
        pack(0, c)
        pieces.append(batch)
    for c in range(2):
        unpack_a(3, z_got, 3, c)
        unpack_a(5, z_got, 5, c)
    for copy in last:
        copy.wait_recv()
    unpack_a(4, z_got, 4, 0)
    unpack_a(4, z_got, 4, 1)

    sign = jnp.where(lax.broadcasted_iota(jnp.int32, (8, CH), 0) < 4, -1.0, 1.0)

    def unpack_e(d, source, chunk):
        n = COUNTS[chunk]
        codes = to_f32(source[d, pl.ds(64 * chunk, 8 * n)])
        scale = jnp.exp2(codes[6 * n :]) * (1.0 / 32767.0)
        at = 24 * d + 16 * chunk
        for k in range(3):
            value = codes[2 * n * k : 2 * n * k + 2 * n] * scale
            flat[2 * k, at : at + 2 * n] = value
            if chunk == 0:
                flat[2 * k + 1, at : at + 8] = -value[8:]
                flat[2 * k + 1, at + 8 : at + 16] = value[:8]
            else:
                flat[2 * k + 1, at : at + 8] = pltpu.roll(value, 4, 0) * sign

    for c in range(2):
        unpack_e(0, piece_send, c)
        for d, copy in pieces[c][::-1]:
            copy.wait_recv()
            unpack_e(d, piece_got, c)
    for k in range(3):
        for part in range(2):
            high, low = split(flat[2 * k + part].T)
            e_op[k, part] = high
            e_op[k, 2 + part] = low

    for n in range(NYL):
        for h in range(2):
            part_val[n, h, 96:] = jnp.zeros((16, CH), jnp.float32)
    row8 = lax.broadcasted_iota(jnp.int32, (8, CH), 0)

    def bins(g, carry):
        rows = pl.ds(pl.multiple_of(JS * g, JS), JS)
        for k in range(3):
            f = 3 * g + k
            high, low = split(a_val[f])
            left_op = jnp.concatenate([e_op[k, n, rows] for n in range(4)], axis=0)
            got = jnp.dot(
                left_op, jnp.concatenate([high, low], axis=1), preferred_element_type=jnp.float32
            )
            got = got[:, :CH] + got[:, CH:]
            got = got[: 2 * JS] + got[2 * JS :]
            tiles = []
            for n in range(2):
                re, im = got[8 * n : 8 * n + 8], got[JS + 8 * n : JS + 8 * n + 8]
                tiles.append(jnp.where(row8 < 4, re, pltpu.roll(im, 4, 0)))
                tiles.append(jnp.where(row8 < 4, pltpu.roll(re, 4, 0), im))
            tops = [jnp.max(jnp.abs(tile), axis=0, keepdims=True) for tile in tiles]
            power = jnp.ceil(jnp.log2(jnp.maximum(jnp.concatenate(tops, axis=0), 1e-30)))
            gain = limit / jnp.exp2(power)
            h, at = g // 4, f % 12
            for n in range(NYL):
                code = jnp.clip(jnp.floor(tiles[n] * gain[n : n + 1] + 0.5), -limit, limit)
                part_val[n, h, pl.ds(pl.multiple_of(8 * at, 8), 8)] = code
                part_val[n, h, pl.ds(96 + at, 1)] = power[n : n + 1]
        return carry

    sums = []
    for h in range(2):
        lax.fori_loop(4 * h, 4 * h + 4, bins, 0)
        for n in range(NYL):
            part_code[n, h] = to_i16(part_val[n, h])
        for e in (2, 1, 3):
            sums.append(
                send(part_code.at[(yl + e) % NYL, h], part_got.at[e - 1, h], at_yl(e))
            )
    norm = 1.0 / math.sqrt(LWIN * NTM)

    def decode(codes):
        values = to_f32(codes)
        scale = jnp.exp2(values[96:108]) * (norm / 32767.0)
        return values[:96].reshape(12, 8, CH) * scale[:, None, :]

    for h in range(2):
        total = decode(part_code[yl, h])
        for copy in sums[3 * h : 3 * h + 3]:
            copy.wait_recv()
        for e in range(NYL - 1):
            total = total + decode(part_got[e, h])
        flat[0, 96 * h : 96 * h + 96] = total.reshape(96, CH)
    for j in range(4):
        for part in range(2):
            rows = flat[0, pl.ds(4 * part + j, NBIN, stride=8), :]
            at = 24 * (2 * j + part)
            flat[1, at : at + 24] = rows
    out_ref[0] = flat[1].T
    for copy in sent:
        copy.wait_send()


def shards(records, fir_taps, partners):
    f32, bf16, i16 = jnp.float32, jnp.bfloat16, jnp.int16
    vmem = pltpu.VMEM
    copies = 55
    return pl.pallas_call(
        kernel,
        out_shape=jax.ShapeDtypeStruct((1, CH, KDIM), f32),
        in_specs=[
            pl.BlockSpec(memory_space=pltpu.SMEM),
            pl.BlockSpec(memory_space=pltpu.VMEM),
            pl.BlockSpec(memory_space=pl.ANY),
            pl.BlockSpec(memory_space=pl.ANY),
        ],
        out_specs=pl.BlockSpec(memory_space=pltpu.VMEM),
        scratch_shapes=[
            vmem((CH, LWIN * HOP), bf16),
            vmem((2 * NQ, WIN + 4 * HALF), bf16),
            vmem((4 * NQ, HOP), bf16),
            vmem((2 * NQ, 128), bf16),
            vmem((2 * NQ, 128), bf16),
            vmem((16, NQ, CH), f32),
            vmem((2, NQ, CH), f32),
            vmem((NQ, CH), f32),
            vmem((2, NQ, CH), f32),
            vmem((NQ, CH), f32),
            vmem((SPEC, CH), f32),
            vmem((8, 400, CH), i16),
            vmem((8, 208, CH), i16),
            vmem((NZ, SPEC, CH), i16),
            vmem((NBIN, KDIM, CH), f32),
            vmem((SPEC, CH), i16),
            vmem((SPEC, CH), i16),
            vmem((NZ, PIECE, CH), i16),
            vmem((NZ, PIECE, CH), i16),
            vmem((3, 4, CH, KDIM), bf16),
            vmem((NYL, 2, 112, CH), f32),
            vmem((NYL, 2, 112, CH), i16),
            vmem((NYL - 1, 2, 112, CH), i16),
            vmem((6, KDIM, CH), f32),
            vmem((NZ, PIECE, CH), f32),
            vmem((1, 512), f32),
            pltpu.SemaphoreType.DMA((6,)),
            pltpu.SemaphoreType.DMA,
            pltpu.SemaphoreType.DMA((copies,)),
            pltpu.SemaphoreType.DMA((copies,)),
        ],
        compiler_params=pltpu.CompilerParams(collective_id=0, has_side_effects=True),
    )(partners, fir_taps, jnp.asarray(basis_table()), records)


def solution(mesh):
    placed = (P("chan", "tm"), P(), P())
    return jax.shard_map(
        shards, mesh=mesh, in_specs=placed, out_specs=P(None, "chan", "tm"), check_vma=False
    )
```

```python
import functools
import math

import jax
import jax.numpy as jnp
import ml_dtypes
import numpy as np
from jax import lax
from jax.experimental import pallas as pl
from jax.experimental.pallas import tpu as pltpu
from jax.sharding import PartitionSpec as P

WIN = 2560
HOP = WIN // 2
NBIN = 24
HALF = 128
FIRST_BIN = 4
NQ = 2 * NBIN
CH = 128
LWIN = 12
SPEC = 608
NX, NYH, NC = 4, 2, 2
NZ, NYL = 8, 4
NTM = NZ * NYL
JS = CH // NZ
PIECE = 96
KDIM = NZ * 2 * LWIN
COUNTS = (8, 4)
BASES = (0, 400)
CHUNKS = (pl.ds(0, 400), pl.ds(400, 208))
HEAD, TAIL = pl.ds(0, 304), pl.ds(304, 96)
BLOCKS = ((0, 80), (80, 80), (160, 80), (240, 80), (320, 80), (400, 112), (512, 96))
MESH = pl.DeviceIdType.MESH
NT = (((1,), (1,)), ((), ()))


def basis_table():
    t = np.arange(WIN)
    edge = np.minimum(t, WIN - 1 - t)
    ramp = np.sin(math.pi * (edge + 0.5) / (2.0 * HALF))
    taper = np.where(edge < HALF, ramp * ramp, 1.0) / math.sqrt(WIN)
    phase = (np.arange(NBIN)[:, None] + FIRST_BIN) * t[None, :] % WIN
    angle = 2.0 * math.pi / WIN * phase
    table = np.concatenate([np.cos(angle), -np.sin(angle)], axis=0) * taper
    table = np.pad(table, ((0, 0), (2 * HALF, 2 * HALF))).astype(np.float32)
    high = table.astype(ml_dtypes.bfloat16)
    low = (table - high.astype(np.float32)).astype(ml_dtypes.bfloat16)
    return np.concatenate([high, low], axis=0)


def split(value):
    high = value.astype(jnp.bfloat16)
    return high, (value - high.astype(jnp.float32)).astype(jnp.bfloat16)


def to_f32(codes):
    return codes.astype(jnp.int32).astype(jnp.float32)


def to_i16(value):
    return value.astype(jnp.int32).astype(jnp.int16)


def kernel(
    partners, taps, basis_hbm, x_hbm, out_ref,
    xs, basis, d_op, e_first, e_last, acc, up_send, low_send, up_recv, low_recv,
    coded, chan_a, chan_b, z_got, a_val, sis_send, sis_recv, piece_send, piece_got,
    e_op, part_val, part_code, part_got, flat, turned, line,
    x_sem, basis_sem, send_sem, recv_sem,
):
    ci, ti = lax.axis_index("chan"), lax.axis_index("tm")
    x, yh, core = ci // 4, (ci // 2) % 2, ci % 2
    z, yl = ti // NYL, ti % NYL

    def chan_id(xx, yy, cc):
        return (xx * 2 + yy) * 2 + cc

    def at_x(step):
        return (chan_id((x + step + NX) % NX, yh, core), ti)

    def at_z(step):
        return (ci, ((z + step + NZ) % NZ) * NYL + yl)

    def at_yl(step):
        return (ci, z * NYL + (yl + step) % NYL)

    def at_tm(step):
        return (ci, (ti + step + NTM) % NTM)

    across = (chan_id(x, 1 - yh, core), ti)
    sister = (chan_id(x, yh, 1 - core), ti)

    fetch_basis = pltpu.make_async_copy(basis_hbm, basis, basis_sem)
    fetch_basis.start()
    pair_order = [0, 5, 1, 2, 3, 4]

    def fetch(p):
        cols = pl.ds(2 * HOP * p, 2 * HOP)
        return pltpu.make_async_copy(x_hbm.at[:, cols], xs.at[:, cols], x_sem.at[p])

    for p in pair_order:
        fetch(p).start()

    barrier = pltpu.get_barrier_semaphore()
    peers = [at_tm(1), at_tm(-1), across, sister, at_x(1), at_x(-1), at_x(2)]
    peers += [at_z(d) for d in range(1, NZ)] + [at_yl(e) for e in range(1, NYL)]
    for peer in peers:
        pl.semaphore_signal(barrier, inc=1, device_id=peer, device_id_type=MESH)

    counter = [0]

    def send(src, dst, device):
        slot = counter[0]
        counter[0] += 1
        copy = pltpu.make_async_remote_copy(
            src_ref=src, dst_ref=dst, send_sem=send_sem.at[slot], recv_sem=recv_sem.at[slot],
            device_id=device, device_id_type=MESH,
        )
        copy.start()
        sent.append(copy)
        return copy

    sent = []

    acc[...] = jnp.zeros_like(acc)
    row = taps[...].astype(jnp.float32).reshape(1, 257)
    line[...] = jnp.zeros_like(line)
    line[:, 256:] = row[:, :256]
    line[:, :1] = row[:, 256:]
    toep = pltpu.roll(jnp.broadcast_to(line[...], (512, 512)), 0, 1, stride=1, stride_axis=0)
    toep = toep[:, :256].astype(jnp.bfloat16)
    fetch_basis.wait()
    for i in range(11):
        both = jnp.dot(
            basis[:, 256 * i : 256 * i + 512], toep, preferred_element_type=jnp.float32
        )
        high, low = split(both[:NQ] + both[NQ:])
        for half in range(2):
            j = 2 * i + half
            h_part = high[:, 128 * half : 128 * half + 128]
            l_part = low[:, 128 * half : 128 * half + 128]
            if j == 0:
                e_last[:NQ, :] = h_part
                e_last[NQ:, :] = l_part
            elif j == 21:
                e_first[:NQ, :] = h_part
                e_first[NQ:, :] = l_part
            else:
                row = 0 if j <= 10 else 2 * NQ
                col = 128 * ((j - 1) % 10)
                d_op[row : row + NQ, col : col + 128] = h_part
                d_op[row + NQ : row + 2 * NQ, col : col + 128] = l_part

    def hop_pair(p):
        fetch(p).wait()
        base = pl.multiple_of(2 * HOP * p, 128)
        second = pl.multiple_of(2 * HOP * p + HOP, 128)
        tail_a = pl.multiple_of(2 * HOP * p + HOP - 128, 128)
        tail_b = pl.multiple_of(2 * HOP * p + 2 * HOP - 128, 128)

        def both_hops(first, other, width):
            return jnp.concatenate([xs[:, pl.ds(first, width)], xs[:, pl.ds(other, width)]], axis=0)

        def product(left, right):
            return lax.dot_general(left, right, NT, preferred_element_type=jnp.float32)

        main = product(d_op[...], both_hops(base, second, HOP))
        first = product(e_first[...], both_hops(base, second, 128))
        last = product(e_last[...], both_hops(tail_a, tail_b, 128))
        p0 = main[:NQ] + main[NQ : 2 * NQ]
        p1 = main[2 * NQ : 3 * NQ] + main[3 * NQ :]
        p2 = first[:NQ] + first[NQ:]
        p3 = last[:NQ] + last[NQ:]
        for hop in range(2):
            lanes = slice(128 * hop, 128 * hop + 128)
            at = 2 * p + hop
            acc[at] += p2[:, lanes]
            acc[at + 1] += p1[:, lanes]
            acc[at + 2] += p0[:, lanes]
            acc[at + 3] += p3[:, lanes]

    hop_pair(0)
    hop_pair(5)
    up_send[...] = acc[0:2]
    low_send[...] = acc[14]
    pl.semaphore_wait(barrier, len(peers))
    up = send(up_send, up_recv, at_tm(-1))
    low = send(low_send, low_recv, at_tm(1))
    pl.loop(1, 5)(hop_pair)

    limit = jnp.float32(32767.0)

    def whiten(w, chunk, i):
        base, n = BASES[chunk], COUNTS[chunk]
        spec = acc[w + 2]
        real, imag = spec[:NBIN], spec[NBIN:]
        amp = jnp.sqrt(real * real + imag * imag + 1.0)
        real, imag = real / amp, imag / amp
        top = jnp.max(jnp.maximum(jnp.abs(real), jnp.abs(imag)), axis=0, keepdims=True)
        power = jnp.ceil(jnp.log2(jnp.maximum(top, 1e-30)))
        gain = limit / jnp.exp2(power)
        for part, value in enumerate((real, imag)):
            code = jnp.clip(jnp.floor(value * gain + 0.5), -limit, limit)
            coded[pl.ds(base + part * n + i, NBIN, stride=2 * n), :] = code
            at = base + NQ * n + part * n + i
            coded[at : at + 1, :] = power

    chan_got = (chan_a, chan_b)

    def chan_slot(dx, dy, chunk):
        return chan_got[chunk].at[2 * dx + dy]

    def launch(chunk):
        rows = CHUNKS[chunk]
        own = chan_slot(0, 0, chunk)
        return [
            send(own, chan_slot(0, 1, chunk), across),
            send(own, z_got.at[2, rows], at_z(2)),
            send(own, z_got.at[6, rows], at_z(-2)),
            send(own, z_got.at[1, rows], at_z(1)),
            send(own, z_got.at[7, rows], at_z(-1)),
            send(own, chan_slot(2, 0, chunk), at_x(2)),
            send(own, chan_slot(1, 0, chunk), at_x(1)),
            send(own, chan_slot(3, 0, chunk), at_x(-1)),
        ]

    for i in range(8):
        whiten(i + 1, 0, i)
    for r, size in BLOCKS[:5]:
        chan_a[0, r : r + size] = to_i16(coded[r : r + size])
    first = launch(0)
    coded[600:, :] = jnp.zeros((8, CH), jnp.float32)
    whiten(9, 1, 1)
    low.wait_recv()
    acc[2] += jnp.where(ti > 0, 1.0, 0.0) * low_recv[...]
    whiten(0, 1, 0)
    up.wait_recv()
    acc[12:14] += jnp.where(ti < NTM - 1, 1.0, 0.0) * up_recv[...]
    whiten(10, 1, 2)
    whiten(11, 1, 3)
    for r, size in BLOCKS[5:]:
        chan_b[0, r - 400 : r - 400 + size] = to_i16(coded[r : r + size])
    second = launch(1)
    own_sent = (first, second)

    def unpack_a(d, source, index, chunk, base=None):
        base, n = BASES[chunk] if base is None else base, COUNTS[chunk]
        at = 16 * d if chunk == 0 else 128 + 8 * d
        power = to_f32(source[index, base + NQ * n : base + NQ * n + 16])
        scale = jnp.exp2(power[: 2 * n]) * (1.0 / 32767.0)
        for i in range(n // 2 * 6):
            block = to_f32(source[index, base + 16 * i : base + 16 * i + 16])
            for k in range(8 // n):
                f = i * (8 // n) + k
                a_val[f, at : at + 2 * n] = block[2 * n * k : 2 * n * k + 2 * n] * scale

    def pass_on(chunk):
        rows = CHUNKS[chunk]
        onward = [
            send(z_got.at[2, rows], z_got.at[3, rows], at_z(1)),
            send(z_got.at[6, rows], z_got.at[5, rows], at_z(-1)),
        ]
        if chunk == 0:
            onward.append(send(z_got.at[2, HEAD], z_got.at[4, HEAD], at_z(2)))
            rows = TAIL
        onward.append(send(z_got.at[6, rows], z_got.at[4, rows], at_z(-2)))
        return onward

    onward, by_x = [], []
    for c in range(2):
        own_sent[c][1].wait_recv()
        own_sent[c][2].wait_recv()
        onward.append(pass_on(c))
        own_sent[c][0].wait_recv()
        came = chan_slot(0, 1, c)
        by_x.append([
            send(came, chan_slot(2, 1, c), at_x(2)),
            send(came, chan_slot(1, 1, c), at_x(1)),
            send(came, chan_slot(3, 1, c), at_x(-1)),
        ])
        unpack_a(0, chan_got[c], 0, c, 0)
        unpack_a(2, z_got, 2, c)
        unpack_a(6, z_got, 6, c)
    for c in range(2):
        for copy in own_sent[c][3:]:
            copy.wait_recv()

    mine_at = partners[0, ci]
    theirs_at = partners[0, chan_id(x, yh, 1 - core)]

    def slot_of(block):
        dx = (x - block // 4 + NX) % NX
        dy = (yh + (block // 2) % 2) % 2
        return 2 * dx + dy

    theirs_slot = slot_of(theirs_at)
    swaps = []
    for c in range(2):
        rows = CHUNKS[c]
        for copy in by_x[c]:
            copy.wait_recv()
        for r, size in BLOCKS[:5] if c == 0 else BLOCKS[5:]:
            at = r - BASES[c]
            sis_send[r : r + size] = chan_got[c][theirs_slot, at : at + size]
        swaps.append(send(sis_send.at[rows], sis_recv.at[rows], sister))
        unpack_a(1, z_got, 1, c)
        unpack_a(7, z_got, 7, c)
    keep = jnp.where(mine_at % 2 == core, 1.0, 0.0)
    other = 1.0 - keep
    mine_slot = slot_of(mine_at)
    shift = (CH - JS * z) % CH

    def pack(d, chunk):
        base, n = BASES[chunk], COUNTS[chunk]
        for r in range(0, 8 * n, 2 * n):
            piece = jnp.zeros((2 * n, CH), jnp.float32)
            group_of = lax.broadcasted_iota(jnp.int32, (2 * n, CH), 1) // JS
            for g in range(NZ):
                row = base + (6 * n * g + r if r < 6 * n else NQ * n)
                moved = coded[row : row + 2 * n]
                if g != d:
                    moved = pltpu.roll(moved, (JS * (g - d) + CH) % CH, 1)
                piece = jnp.where(group_of == g, moved, piece)
            at = 64 * chunk + r
            turned[d, at : at + 2 * n] = piece
        rows = pl.ds(64 * chunk, 8 * n)
        piece_send[d, rows] = to_i16(turned[d, rows])

    pieces = []
    for c in range(2):
        swaps[c].wait_recv()
        for r, size in BLOCKS[:5] if c == 0 else BLOCKS[5:]:
            at = r - BASES[c]
            picked = to_f32(chan_got[c][mine_slot, at : at + size]) * keep
            picked = picked + to_f32(sis_recv[r : r + size]) * other
            coded[r : r + size] = pltpu.roll(picked, shift, 1)
        rows = pl.ds(64 * c, 8 * COUNTS[c])
        batch = []
        for d in (4, 3, 5, 2, 6, 1, 7):
            pack(d, c)
            batch.append((d, send(piece_send.at[d, rows], piece_got.at[d, rows], at_z(d))))
        pack(0, c)
        pieces.append(batch)
    for c in range(2):
        for copy in onward[c]:
            copy.wait_recv()
        for d in (3, 5, 4):
            unpack_a(d, z_got, d, c)

    sign = jnp.where(lax.broadcasted_iota(jnp.int32, (8, CH), 0) < 4, -1.0, 1.0)

    def unpack_e(d, source, chunk):
        n = COUNTS[chunk]
        codes = to_f32(source[d, pl.ds(64 * chunk, 8 * n)])
        scale = jnp.exp2(codes[6 * n :]) * (1.0 / 32767.0)
        at = 16 * d if chunk == 0 else 128 + 8 * d
        for k in range(3):
            value = codes[2 * n * k : 2 * n * k + 2 * n] * scale
            flat[2 * k, at : at + 2 * n] = value
            if chunk == 0:
                flat[2 * k + 1, at : at + 8] = -value[8:]
                flat[2 * k + 1, at + 8 : at + 16] = value[:8]
            else:
                flat[2 * k + 1, at : at + 8] = pltpu.roll(value, 4, 0) * sign

    for c in range(2):
        unpack_e(0, piece_send, c)
        for d, copy in pieces[c][::-1]:
            copy.wait_recv()
            unpack_e(d, piece_got, c)
        depth = slice(0, 128) if c == 0 else slice(128, KDIM)
        for k in range(3):
            for part in range(2):
                high, low = split(flat[2 * k + part, depth].T)
                e_op[k, part, :, depth] = high
                e_op[k, 2 + part, :, depth] = low

    for n in range(NYL):
        for h in range(2):
            part_val[n, h, 96:] = jnp.zeros((16, CH), jnp.float32)
    row8 = lax.broadcasted_iota(jnp.int32, (8, CH), 0)

    def bins(g, carry):
        rows = pl.ds(pl.multiple_of(JS * g, JS), JS)
        for k in range(3):
            f = 3 * g + k
            high, low = split(a_val[f])
            left_op = jnp.concatenate([e_op[k, n, rows] for n in range(4)], axis=0)
            got = jnp.dot(
                left_op, jnp.concatenate([high, low], axis=1), preferred_element_type=jnp.float32
            )
            got = got[:, :CH] + got[:, CH:]
            got = got[: 2 * JS] + got[2 * JS :]
            tiles = []
            for n in range(2):
                re, im = got[8 * n : 8 * n + 8], got[JS + 8 * n : JS + 8 * n + 8]
                tiles.append(jnp.where(row8 < 4, re, pltpu.roll(im, 4, 0)))
                tiles.append(jnp.where(row8 < 4, pltpu.roll(re, 4, 0), im))
            tops = [jnp.max(jnp.abs(tile), axis=0, keepdims=True) for tile in tiles]
            power = jnp.ceil(jnp.log2(jnp.maximum(jnp.concatenate(tops, axis=0), 1e-30)))
            gain = limit / jnp.exp2(power)
            h, at = g // 4, f % 12
            for n in range(NYL):
                code = jnp.clip(jnp.floor(tiles[n] * gain[n : n + 1] + 0.5), -limit, limit)
                part_val[n, h, pl.ds(pl.multiple_of(8 * at, 8), 8)] = code
                part_val[n, h, pl.ds(96 + at, 1)] = power[n : n + 1]
        return carry

    sums = []
    for h in range(2):
        lax.fori_loop(4 * h, 4 * h + 4, bins, 0)
        for n in range(NYL):
            part_code[n, h] = to_i16(part_val[n, h])
        for e in (2, 1, 3):
            sums.append(
                send(part_code.at[(yl + e) % NYL, h], part_got.at[e - 1, h], at_yl(e))
            )
    norm = 1.0 / math.sqrt(LWIN * NTM)

    def decode(codes):
        values = to_f32(codes)
        scale = jnp.exp2(values[96:108]) * (norm / 32767.0)
        return values[:96].reshape(12, 8, CH) * scale[:, None, :]

    for h in range(2):
        total = decode(part_code[yl, h])
        for copy in sums[3 * h : 3 * h + 3]:
            copy.wait_recv()
        for e in range(NYL - 1):
            total = total + decode(part_got[e, h])
        flat[0, 96 * h : 96 * h + 96] = total.reshape(96, CH)
    for j in range(4):
        for part in range(2):
            rows = flat[0, pl.ds(4 * part + j, NBIN, stride=8), :]
            at = 24 * (2 * j + part)
            flat[1, at : at + 24] = rows
    out_ref[0] = flat[1].T
    for copy in sent:
        copy.wait_send()


def shards(records, fir_taps, partners):
    f32, bf16, i16 = jnp.float32, jnp.bfloat16, jnp.int16
    vmem = pltpu.VMEM
    copies = 55
    return pl.pallas_call(
        kernel,
        out_shape=jax.ShapeDtypeStruct((1, CH, KDIM), f32),
        in_specs=[
            pl.BlockSpec(memory_space=pltpu.SMEM),
            pl.BlockSpec(memory_space=pltpu.VMEM),
            pl.BlockSpec(memory_space=pl.ANY),
            pl.BlockSpec(memory_space=pl.ANY),
        ],
        out_specs=pl.BlockSpec(memory_space=pltpu.VMEM),
        scratch_shapes=[
            vmem((CH, LWIN * HOP), bf16),
            vmem((2 * NQ, WIN + 4 * HALF), bf16),
            vmem((4 * NQ, HOP), bf16),
            vmem((2 * NQ, 128), bf16),
            vmem((2 * NQ, 128), bf16),
            vmem((16, NQ, CH), f32),
            vmem((2, NQ, CH), f32),
            vmem((NQ, CH), f32),
            vmem((2, NQ, CH), f32),
            vmem((NQ, CH), f32),
            vmem((SPEC, CH), f32),
            vmem((8, 400, CH), i16),
            vmem((8, 208, CH), i16),
            vmem((NZ, SPEC, CH), i16),
            vmem((NBIN, KDIM, CH), f32),
            vmem((SPEC, CH), i16),
            vmem((SPEC, CH), i16),
            vmem((NZ, PIECE, CH), i16),
            vmem((NZ, PIECE, CH), i16),
            vmem((3, 4, CH, KDIM), bf16),
            vmem((NYL, 2, 112, CH), f32),
            vmem((NYL, 2, 112, CH), i16),
            vmem((NYL - 1, 2, 112, CH), i16),
            vmem((6, KDIM, CH), f32),
            vmem((NZ, PIECE, CH), f32),
            vmem((1, 512), f32),
            pltpu.SemaphoreType.DMA((6,)),
            pltpu.SemaphoreType.DMA,
            pltpu.SemaphoreType.DMA((copies,)),
            pltpu.SemaphoreType.DMA((copies,)),
        ],
        compiler_params=pltpu.CompilerParams(collective_id=0, has_side_effects=True),
    )(partners, fir_taps, jnp.asarray(basis_table()), records)


def solution(mesh):
    placed = (P("chan", "tm"), P(), P())
    return jax.shard_map(
        shards, mesh=mesh, in_specs=placed, out_specs=P(None, "chan", "tm"), check_vma=False
    )
```

```python
import functools
import math

import jax
import jax.numpy as jnp
import ml_dtypes
import numpy as np
from jax import lax
from jax.experimental import pallas as pl
from jax.experimental.pallas import tpu as pltpu
from jax.sharding import PartitionSpec as P

WIN = 2560
HOP = WIN // 2
NBIN = 24
HALF = 128
FIRST_BIN = 4
NQ = 2 * NBIN
CH = 128
LWIN = 12
SPEC = 608
NX, NYH, NC = 4, 2, 2
NZ, NYL = 8, 4
NTM = NZ * NYL
JS = CH // NZ
PIECE = 96
KDIM = NZ * 2 * LWIN
COUNTS = (8, 4)
BASES = (0, 400)
CHUNKS = (pl.ds(0, 400), pl.ds(400, 208))
DEPTHS = (slice(0, 128), slice(128, 192))
HEAD, TAIL = pl.ds(0, 304), pl.ds(304, 96)
BLOCKS = ((0, 80), (80, 80), (160, 80), (240, 80), (320, 80), (400, 112), (512, 96))
MESH = pl.DeviceIdType.MESH
NT = (((1,), (1,)), ((), ()))


def basis_table():
    t = np.arange(WIN)
    edge = np.minimum(t, WIN - 1 - t)
    ramp = np.sin(math.pi * (edge + 0.5) / (2.0 * HALF))
    taper = np.where(edge < HALF, ramp * ramp, 1.0) / math.sqrt(WIN)
    phase = (np.arange(NBIN)[:, None] + FIRST_BIN) * t[None, :] % WIN
    angle = 2.0 * math.pi / WIN * phase
    table = np.concatenate([np.cos(angle), -np.sin(angle)], axis=0) * taper
    table = np.pad(table, ((0, 0), (2 * HALF, 2 * HALF))).astype(np.float32)
    high = table.astype(ml_dtypes.bfloat16)
    low = (table - high.astype(np.float32)).astype(ml_dtypes.bfloat16)
    return np.concatenate([high, low], axis=0)


def split(value):
    high = value.astype(jnp.bfloat16)
    return high, (value - high.astype(jnp.float32)).astype(jnp.bfloat16)


def to_f32(codes):
    return codes.astype(jnp.int32).astype(jnp.float32)


def to_i16(value):
    return value.astype(jnp.int32).astype(jnp.int16)


def kernel(
    partners, taps, basis_hbm, x_hbm, out_ref,
    xs, basis, d_op, e_first, e_last, acc, up_send, low_send, up_recv, low_recv,
    coded, chan_a, chan_b, z_got, a_val, sis_send, sis_recv, piece_send, piece_got,
    e_op, part_val, part_code, part_got, flat, turned, line, a_op, early,
    x_sem, basis_sem, send_sem, recv_sem,
):
    ci, ti = lax.axis_index("chan"), lax.axis_index("tm")
    x, yh, core = ci // 4, (ci // 2) % 2, ci % 2
    z, yl = ti // NYL, ti % NYL

    def chan_id(xx, yy, cc):
        return (xx * 2 + yy) * 2 + cc

    def at_x(step):
        return (chan_id((x + step + NX) % NX, yh, core), ti)

    def at_z(step):
        return (ci, ((z + step + NZ) % NZ) * NYL + yl)

    def at_yl(step):
        return (ci, z * NYL + (yl + step) % NYL)

    def at_tm(step):
        return (ci, (ti + step + NTM) % NTM)

    across = (chan_id(x, 1 - yh, core), ti)
    sister = (chan_id(x, yh, 1 - core), ti)

    fetch_basis = pltpu.make_async_copy(basis_hbm, basis, basis_sem)
    fetch_basis.start()
    pair_order = [0, 5, 1, 2, 3, 4]

    def fetch(p):
        cols = pl.ds(2 * HOP * p, 2 * HOP)
        return pltpu.make_async_copy(x_hbm.at[:, cols], xs.at[:, cols], x_sem.at[p])

    for p in pair_order:
        fetch(p).start()

    barrier = pltpu.get_barrier_semaphore()
    peers = [at_tm(1), at_tm(-1), across, sister, at_x(1), at_x(-1), at_x(2)]
    peers += [at_z(d) for d in range(1, NZ)] + [at_yl(e) for e in range(1, NYL)]
    for peer in peers:
        pl.semaphore_signal(barrier, inc=1, device_id=peer, device_id_type=MESH)

    counter = [0]

    def send(src, dst, device):
        slot = counter[0]
        counter[0] += 1
        copy = pltpu.make_async_remote_copy(
            src_ref=src, dst_ref=dst, send_sem=send_sem.at[slot], recv_sem=recv_sem.at[slot],
            device_id=device, device_id_type=MESH,
        )
        copy.start()
        sent.append(copy)
        return copy

    sent = []

    acc[...] = jnp.zeros_like(acc)
    row = taps[...].astype(jnp.float32).reshape(1, 257)
    line[...] = jnp.zeros_like(line)
    line[:, 256:] = row[:, :256]
    line[:, :1] = row[:, 256:]
    toep = pltpu.roll(jnp.broadcast_to(line[...], (512, 512)), 0, 1, stride=1, stride_axis=0)
    toep = toep[:, :256].astype(jnp.bfloat16)
    fetch_basis.wait()
    for i in range(11):
        both = jnp.dot(
            basis[:, 256 * i : 256 * i + 512], toep, preferred_element_type=jnp.float32
        )
        high, low = split(both[:NQ] + both[NQ:])
        for half in range(2):
            j = 2 * i + half
            h_part = high[:, 128 * half : 128 * half + 128]
            l_part = low[:, 128 * half : 128 * half + 128]
            if j == 0:
                e_last[:NQ, :] = h_part
                e_last[NQ:, :] = l_part
            elif j == 21:
                e_first[:NQ, :] = h_part
                e_first[NQ:, :] = l_part
            else:
                row = 0 if j <= 10 else 2 * NQ
                col = 128 * ((j - 1) % 10)
                d_op[row : row + NQ, col : col + 128] = h_part
                d_op[row + NQ : row + 2 * NQ, col : col + 128] = l_part

    def hop_pair(p):
        fetch(p).wait()
        base = pl.multiple_of(2 * HOP * p, 128)
        second = pl.multiple_of(2 * HOP * p + HOP, 128)
        tail_a = pl.multiple_of(2 * HOP * p + HOP - 128, 128)
        tail_b = pl.multiple_of(2 * HOP * p + 2 * HOP - 128, 128)

        def both_hops(first, other, width):
            return jnp.concatenate([xs[:, pl.ds(first, width)], xs[:, pl.ds(other, width)]], axis=0)

        def product(left, right):
            return lax.dot_general(left, right, NT, preferred_element_type=jnp.float32)

        main = product(d_op[...], both_hops(base, second, HOP))
        first = product(e_first[...], both_hops(base, second, 128))
        last = product(e_last[...], both_hops(tail_a, tail_b, 128))
        p0 = main[:NQ] + main[NQ : 2 * NQ]
        p1 = main[2 * NQ : 3 * NQ] + main[3 * NQ :]
        p2 = first[:NQ] + first[NQ:]
        p3 = last[:NQ] + last[NQ:]
        for hop in range(2):
            lanes = slice(128 * hop, 128 * hop + 128)
            at = 2 * p + hop
            acc[at] += p2[:, lanes]
            acc[at + 1] += p1[:, lanes]
            acc[at + 2] += p0[:, lanes]
            acc[at + 3] += p3[:, lanes]

    hop_pair(0)
    hop_pair(5)
    up_send[...] = acc[0:2]
    low_send[...] = acc[14]
    pl.semaphore_wait(barrier, len(peers))
    up = send(up_send, up_recv, at_tm(-1))
    low = send(low_send, low_recv, at_tm(1))
    pl.loop(1, 5)(hop_pair)

    limit = jnp.float32(32767.0)

    def whiten(w, chunk, i):
        base, n = BASES[chunk], COUNTS[chunk]
        spec = acc[w + 2]
        real, imag = spec[:NBIN], spec[NBIN:]
        amp = jnp.sqrt(real * real + imag * imag + 1.0)
        real, imag = real / amp, imag / amp
        top = jnp.max(jnp.maximum(jnp.abs(real), jnp.abs(imag)), axis=0, keepdims=True)
        power = jnp.ceil(jnp.log2(jnp.maximum(top, 1e-30)))
        gain = limit / jnp.exp2(power)
        for part, value in enumerate((real, imag)):
            code = jnp.clip(jnp.floor(value * gain + 0.5), -limit, limit)
            coded[pl.ds(base + part * n + i, NBIN, stride=2 * n), :] = code
            at = base + NQ * n + part * n + i
            coded[at : at + 1, :] = power

    chan_got = (chan_a, chan_b)

    def chan_slot(dx, dy, chunk):
        return chan_got[chunk].at[2 * dx + dy]

    def launch(chunk):
        rows = CHUNKS[chunk]
        own = chan_slot(0, 0, chunk)
        return [
            send(own, chan_slot(0, 1, chunk), across),
            send(own, z_got.at[2, rows], at_z(2)),
            send(own, z_got.at[6, rows], at_z(-2)),
            send(own, z_got.at[1, rows], at_z(1)),
            send(own, z_got.at[7, rows], at_z(-1)),
            send(own, chan_slot(2, 0, chunk), at_x(2)),
            send(own, chan_slot(1, 0, chunk), at_x(1)),
            send(own, chan_slot(3, 0, chunk), at_x(-1)),
        ]

    for i in range(8):
        whiten(i + 1, 0, i)
    for r, size in BLOCKS[:5]:
        chan_a[0, r : r + size] = to_i16(coded[r : r + size])
    first = launch(0)
    coded[600:, :] = jnp.zeros((8, CH), jnp.float32)
    whiten(9, 1, 1)
    low.wait_recv()
    acc[2] += jnp.where(ti > 0, 1.0, 0.0) * low_recv[...]
    whiten(0, 1, 0)
    up.wait_recv()
    acc[12:14] += jnp.where(ti < NTM - 1, 1.0, 0.0) * up_recv[...]
    whiten(10, 1, 2)
    whiten(11, 1, 3)
    for r, size in BLOCKS[5:]:
        chan_b[0, r - 400 : r - 400 + size] = to_i16(coded[r : r + size])
    second = launch(1)
    own_sent = (first, second)

    def unpack_a(d, source, index, chunk, base=None):
        base, n = BASES[chunk] if base is None else base, COUNTS[chunk]
        at = 16 * d if chunk == 0 else 128 + 8 * d
        power = to_f32(source[index, base + NQ * n : base + NQ * n + 16])
        scale = jnp.exp2(power[: 2 * n]) * (1.0 / 32767.0)
        for i in range(n // 2 * 6):
            block = to_f32(source[index, base + 16 * i : base + 16 * i + 16])
            for k in range(8 // n):
                f = i * (8 // n) + k
                a_val[f, at : at + 2 * n] = block[2 * n * k : 2 * n * k + 2 * n] * scale

    def pass_on(chunk):
        rows = CHUNKS[chunk]
        onward = [
            send(z_got.at[2, rows], z_got.at[3, rows], at_z(1)),
            send(z_got.at[6, rows], z_got.at[5, rows], at_z(-1)),
        ]
        if chunk == 0:
            onward.append(send(z_got.at[2, HEAD], z_got.at[4, HEAD], at_z(2)))
            rows = TAIL
        onward.append(send(z_got.at[6, rows], z_got.at[4, rows], at_z(-2)))
        return onward

    onward, by_x = [], []
    for c in range(2):
        own_sent[c][1].wait_recv()
        own_sent[c][2].wait_recv()
        onward.append(pass_on(c))
        own_sent[c][0].wait_recv()
        came = chan_slot(0, 1, c)
        by_x.append([
            send(came, chan_slot(2, 1, c), at_x(2)),
            send(came, chan_slot(1, 1, c), at_x(1)),
            send(came, chan_slot(3, 1, c), at_x(-1)),
        ])
        unpack_a(0, chan_got[c], 0, c, 0)
        unpack_a(2, z_got, 2, c)
        unpack_a(6, z_got, 6, c)
    for c in range(2):
        for copy in own_sent[c][3:]:
            copy.wait_recv()

    mine_at = partners[0, ci]
    theirs_at = partners[0, chan_id(x, yh, 1 - core)]

    def slot_of(block):
        dx = (x - block // 4 + NX) % NX
        dy = (yh + (block // 2) % 2) % 2
        return 2 * dx + dy

    theirs_slot = slot_of(theirs_at)
    swaps = []
    for c in range(2):
        rows = CHUNKS[c]
        for copy in by_x[c]:
            copy.wait_recv()
        for r, size in BLOCKS[:5] if c == 0 else BLOCKS[5:]:
            at = r - BASES[c]
            sis_send[r : r + size] = chan_got[c][theirs_slot, at : at + size]
        swaps.append(send(sis_send.at[rows], sis_recv.at[rows], sister))
        unpack_a(1, z_got, 1, c)
        unpack_a(7, z_got, 7, c)
    keep = jnp.where(mine_at % 2 == core, 1.0, 0.0)
    other = 1.0 - keep
    mine_slot = slot_of(mine_at)
    shift = (CH - JS * z) % CH

    def pack(d, chunk):
        base, n = BASES[chunk], COUNTS[chunk]
        for r in range(0, 8 * n, 2 * n):
            piece = jnp.zeros((2 * n, CH), jnp.float32)
            group_of = lax.broadcasted_iota(jnp.int32, (2 * n, CH), 1) // JS
            for g in range(NZ):
                row = base + (6 * n * g + r if r < 6 * n else NQ * n)
                moved = coded[row : row + 2 * n]
                if g != d:
                    moved = pltpu.roll(moved, (JS * (g - d) + CH) % CH, 1)
                piece = jnp.where(group_of == g, moved, piece)
            at = 64 * chunk + r
            turned[d, at : at + 2 * n] = piece
        rows = pl.ds(64 * chunk, 8 * n)
        piece_send[d, rows] = to_i16(turned[d, rows])

    pieces = []
    for c in range(2):
        swaps[c].wait_recv()
        for r, size in BLOCKS[:5] if c == 0 else BLOCKS[5:]:
            at = r - BASES[c]
            picked = to_f32(chan_got[c][mine_slot, at : at + size]) * keep
            picked = picked + to_f32(sis_recv[r : r + size]) * other
            coded[r : r + size] = pltpu.roll(picked, shift, 1)
        rows = pl.ds(64 * c, 8 * COUNTS[c])
        batch = []
        for d in (4, 3, 5, 2, 6, 1, 7):
            pack(d, c)
            batch.append((d, send(piece_send.at[d, rows], piece_got.at[d, rows], at_z(d))))
        pack(0, c)
        pieces.append(batch)
    for c in range(2):
        for copy in onward[c]:
            copy.wait_recv()
        for d in (3, 5, 4):
            unpack_a(d, z_got, d, c)
        depth = DEPTHS[c]

        def halve(f, carry):
            high, low = split(a_val[f, depth])
            a_op[f, depth, :CH] = high
            a_op[f, depth, CH:] = low
            return carry

        lax.fori_loop(0, NBIN, halve, 0)

    def product(g, k, depth):
        rows = pl.ds(pl.multiple_of(JS * g, JS), JS)
        left_op = jnp.concatenate([e_op[k, n, rows, depth] for n in range(4)], axis=0)
        got = jnp.dot(left_op, a_op[3 * g + k, depth], preferred_element_type=jnp.float32)
        got = got[:, :CH] + got[:, CH:]
        return got[: 2 * JS] + got[2 * JS :]

    def first_bins(g, carry):
        for k in range(3):
            early[3 * g + k] = product(g, k, DEPTHS[0])
        return carry

    sign = jnp.where(lax.broadcasted_iota(jnp.int32, (8, CH), 0) < 4, -1.0, 1.0)

    def unpack_e(d, source, chunk):
        n = COUNTS[chunk]
        codes = to_f32(source[d, pl.ds(64 * chunk, 8 * n)])
        scale = jnp.exp2(codes[6 * n :]) * (1.0 / 32767.0)
        at = 16 * d if chunk == 0 else 128 + 8 * d
        for k in range(3):
            value = codes[2 * n * k : 2 * n * k + 2 * n] * scale
            flat[2 * k, at : at + 2 * n] = value
            if chunk == 0:
                flat[2 * k + 1, at : at + 8] = -value[8:]
                flat[2 * k + 1, at + 8 : at + 16] = value[:8]
            else:
                flat[2 * k + 1, at : at + 8] = pltpu.roll(value, 4, 0) * sign

    for c in range(2):
        unpack_e(0, piece_send, c)
        for d, copy in pieces[c][::-1]:
            copy.wait_recv()
            unpack_e(d, piece_got, c)
        depth = DEPTHS[c]
        for k in range(3):
            for part in range(2):
                high, low = split(flat[2 * k + part, depth].T)
                e_op[k, part, :, depth] = high
                e_op[k, 2 + part, :, depth] = low
        if c == 0:
            lax.fori_loop(0, NZ, first_bins, 0)

    for n in range(NYL):
        for h in range(2):
            part_val[n, h, 96:] = jnp.zeros((16, CH), jnp.float32)
    row8 = lax.broadcasted_iota(jnp.int32, (8, CH), 0)

    def bins(g, carry):
        for k in range(3):
            f = 3 * g + k
            got = early[f] + product(g, k, DEPTHS[1])
            tiles = []
            for n in range(2):
                re, im = got[8 * n : 8 * n + 8], got[JS + 8 * n : JS + 8 * n + 8]
                tiles.append(jnp.where(row8 < 4, re, pltpu.roll(im, 4, 0)))
                tiles.append(jnp.where(row8 < 4, pltpu.roll(re, 4, 0), im))
            tops = [jnp.max(jnp.abs(tile), axis=0, keepdims=True) for tile in tiles]
            power = jnp.ceil(jnp.log2(jnp.maximum(jnp.concatenate(tops, axis=0), 1e-30)))
            gain = limit / jnp.exp2(power)
            h, at = g // 4, f % 12
            for n in range(NYL):
                code = jnp.clip(jnp.floor(tiles[n] * gain[n : n + 1] + 0.5), -limit, limit)
                part_val[n, h, pl.ds(pl.multiple_of(8 * at, 8), 8)] = code
                part_val[n, h, pl.ds(96 + at, 1)] = power[n : n + 1]
        return carry

    sums = []
    for h in range(2):
        lax.fori_loop(4 * h, 4 * h + 4, bins, 0)
        for n in range(NYL):
            part_code[n, h] = to_i16(part_val[n, h])
        for e in (2, 1, 3):
            sums.append(
                send(part_code.at[(yl + e) % NYL, h], part_got.at[e - 1, h], at_yl(e))
            )
    norm = 1.0 / math.sqrt(LWIN * NTM)

    def decode(codes):
        values = to_f32(codes)
        scale = jnp.exp2(values[96:108]) * (norm / 32767.0)
        return values[:96].reshape(12, 8, CH) * scale[:, None, :]

    for h in range(2):
        total = decode(part_code[yl, h])
        for copy in sums[3 * h : 3 * h + 3]:
            copy.wait_recv()
        for e in range(NYL - 1):
            total = total + decode(part_got[e, h])
        flat[0, 96 * h : 96 * h + 96] = total.reshape(96, CH)
    for j in range(4):
        for part in range(2):
            rows = flat[0, pl.ds(4 * part + j, NBIN, stride=8), :]
            at = 24 * (2 * j + part)
            flat[1, at : at + 24] = rows
    out_ref[0] = flat[1].T
    for copy in sent:
        copy.wait_send()


def shards(records, fir_taps, partners):
    f32, bf16, i16 = jnp.float32, jnp.bfloat16, jnp.int16
    vmem = pltpu.VMEM
    copies = 55
    return pl.pallas_call(
        kernel,
        out_shape=jax.ShapeDtypeStruct((1, CH, KDIM), f32),
        in_specs=[
            pl.BlockSpec(memory_space=pltpu.SMEM),
            pl.BlockSpec(memory_space=pltpu.VMEM),
            pl.BlockSpec(memory_space=pl.ANY),
            pl.BlockSpec(memory_space=pl.ANY),
        ],
        out_specs=pl.BlockSpec(memory_space=pltpu.VMEM),
        scratch_shapes=[
            vmem((CH, LWIN * HOP), bf16),
            vmem((2 * NQ, WIN + 4 * HALF), bf16),
            vmem((4 * NQ, HOP), bf16),
            vmem((2 * NQ, 128), bf16),
            vmem((2 * NQ, 128), bf16),
            vmem((16, NQ, CH), f32),
            vmem((2, NQ, CH), f32),
            vmem((NQ, CH), f32),
            vmem((2, NQ, CH), f32),
            vmem((NQ, CH), f32),
            vmem((SPEC, CH), f32),
            vmem((8, 400, CH), i16),
            vmem((8, 208, CH), i16),
            vmem((NZ, SPEC, CH), i16),
            vmem((NBIN, KDIM, CH), f32),
            vmem((SPEC, CH), i16),
            vmem((SPEC, CH), i16),
            vmem((NZ, PIECE, CH), i16),
            vmem((NZ, PIECE, CH), i16),
            vmem((3, 4, CH, KDIM), bf16),
            vmem((NYL, 2, 112, CH), f32),
            vmem((NYL, 2, 112, CH), i16),
            vmem((NYL - 1, 2, 112, CH), i16),
            vmem((6, KDIM, CH), f32),
            vmem((NZ, PIECE, CH), f32),
            vmem((1, 512), f32),
            vmem((NBIN, KDIM, 2 * CH), bf16),
            vmem((NBIN, 2 * JS, CH), f32),
            pltpu.SemaphoreType.DMA((6,)),
            pltpu.SemaphoreType.DMA,
            pltpu.SemaphoreType.DMA((copies,)),
            pltpu.SemaphoreType.DMA((copies,)),
        ],
        compiler_params=pltpu.CompilerParams(collective_id=0, has_side_effects=True),
    )(partners, fir_taps, jnp.asarray(basis_table()), records)


def solution(mesh):
    placed = (P("chan", "tm"), P(), P())
    return jax.shard_map(
        shards, mesh=mesh, in_specs=placed, out_specs=P(None, "chan", "tm"), check_vma=False
    )
```
